32 devices in a mesh: seq: 8 (over z, y), chan: 4 (over x, core).
Axes of the slice: x: 2, y: 2, z: 4, core: 2. Of those that a mesh axis runs over, the one named last changes fastest.
Arguments:
- value: bfloat16 [1024, 4096], P('seq', 'chan'), may hold values from -6 to 6
- gate: bfloat16 [1024, 4096], P('seq', 'chan'), may hold values from -6 to 6
- long_filter: bfloat16 [4096, 1024], P('chan', 'seq'), may hold values from -0.5 to 0.5
- skip_gain: float32 [4096], P('chan'), may hold values from 0.5 to 2
- cotangent: bfloat16 [1024, 4096], P('seq', 'chan'), may hold values from -6 to 6
- owner_map: int32 [8], replicated, may hold values from 0 to 7, each once
Outputs:
- output: bfloat16 [1024, 4096], P('seq', 'chan')
- value_grad: bfloat16 [1024, 4096], P('seq', 'chan')
- gate_grad: bfloat16 [1024, 4096], P('seq', 'chan')
- gain_grad: float32 [4, 8, 128], P('chan', 'seq')
The draws below stay inside these ranges and needn't reach their ends.
Inputs may be any that keep to these rules, and one draw needn't show every extreme that they name: `owner_map`: a permutation: each index of seq once.
All inputs are finite; a program needn't handle non-finite values.
Results may differ from the reference program's by a relative error of at most 0.008.
Values may be sent and summed in bfloat16 or wider, within the bound.
A program may use at most 64 MiB of HBM per device.

```python
import math
import jax
import jax.numpy as jnp
from jax import lax

C = 4096
SEQ_LEN = 1024
BLOCK_ROWS = 128
N_SEQ = 8
N_CHAN = 4


def block_scale(key, shape, shards, smallest, top_value):
    loudness, own = 1.0, jax.random.fold_in(key, 6)
    for dim, blocks in shards:
        steps = jnp.exp(jax.random.uniform(jax.random.fold_in(own, dim), (blocks,), jnp.float32, smallest / len(shards), top_value / len(shards)))
        loudness = loudness * jnp.repeat(steps, shape[dim] // blocks).reshape([-1 if axis == dim else 1 for axis in range(len(shape))])
    return loudness


def centred(stream_key, shape, spread, reach, cuts=(), kind=jnp.bfloat16):
    entries = jax.random.normal(stream_key, shape, jnp.float32) * spread
    if len(cuts) > 0:
        entries = block_scale(stream_key, shape, cuts, -0.22, 0.18) * entries
    return jnp.clip(entries, min=-reach, max=reach).astype(kind)


def setup_inputs(seed: int = 0) -> dict:
    arg_keys = jax.random.split(jax.random.key(seed), 7)
    value = centred(arg_keys[0], (SEQ_LEN, C), 1.0, 6.0, ((0, 8), (1, 4)))
    gate = centred(arg_keys[1], (SEQ_LEN, C), 1.0, 6.0, ((0, 8), (1, 4)))
    long_filter = centred(arg_keys[2], (C, SEQ_LEN), (SEQ_LEN ** -0.5), 0.5, ((0, 4), (1, 8)))
    skip_gain = jnp.clip(0.5 + 1.5 * jax.random.uniform(arg_keys[3], (C,), jnp.float32) ** block_scale(arg_keys[3], (C,), ((0, 4),), -0.2, 0.2), 0.5, 2.0)
    cotangent = centred(arg_keys[4], (SEQ_LEN, C), 1.0, 6.0, ((0, 8), (1, 4)))
    owner_map = jax.random.permutation(arg_keys[5], N_SEQ).astype(jnp.int32)
    return dict(value=value, gate=gate, long_filter=long_filter, skip_gain=skip_gain, cotangent=cotangent, owner_map=owner_map)


def reference(value, gate, long_filter, skip_gain, cotangent, owner_map):
    length = value.shape[0]
    value_f = value.astype(jnp.float32)
    gate_f = gate.astype(jnp.float32)
    grad_conv = (cotangent.astype(jnp.float32) * gate_f).astype(jnp.bfloat16)
    padded = 2 * length
    filter_spec = jnp.fft.rfft(long_filter.astype(jnp.float32), n=padded, axis=1)
    value_spec = jnp.fft.rfft(value_f.T, n=padded, axis=1)
    conv = jnp.fft.irfft(value_spec * filter_spec, n=padded, axis=1)[:, :length].astype(jnp.bfloat16)
    grad_spec = jnp.fft.rfft(grad_conv.astype(jnp.float32).T, n=padded, axis=1)
    back_conv = jnp.fft.irfft(grad_spec * jnp.conj(filter_spec), n=padded, axis=1)[:, :length].astype(jnp.bfloat16)
    mixed = conv.T.astype(jnp.float32) + skip_gain * value_f
    output = (gate_f * mixed).astype(jnp.bfloat16)
    gate_grad = (cotangent.astype(jnp.float32) * mixed).astype(jnp.bfloat16)
    value_grad = (back_conv.T.astype(jnp.float32) + skip_gain * grad_conv.astype(jnp.float32)).astype(jnp.bfloat16)
    scale = 1.0 / math.sqrt(length)
    skip_grad = lax.optimization_barrier(jnp.sum(value_f * grad_conv.astype(jnp.float32), axis=0)) * scale
    blocked = skip_grad.reshape(N_CHAN, N_SEQ, BLOCK_ROWS)
    gain_grad = jnp.take(blocked, owner_map.astype(jnp.int32), axis=1)
    return (output, value_grad, gate_grad, gain_grad)
```

```python
import functools
import math

import jax
import jax.numpy as jnp
import numpy as np
from jax import lax
from jax.experimental import pallas as pl
from jax.experimental.pallas import tpu as pltpu
from jax.sharding import PartitionSpec as P

HIGHEST = lax.Precision.HIGHEST


def dft_table(size):
    index = jnp.arange(size, dtype=jnp.int32)
    phase = index[:, None] * index[None, :] % size
    angle = 2.0 * math.pi / size * phase.astype(jnp.float32)
    return (jnp.cos(angle), jnp.sin(angle))


def make_tables(outer, inner):
    cos_outer, sin_outer = dft_table(outer)
    cos_inner, sin_inner = dft_table(inner)
    total = outer * inner
    phase = (
        jnp.arange(outer, dtype=jnp.int32)[:, None]
        * jnp.arange(inner, dtype=jnp.int32)[None, :]
        % total
    )
    angle = 2.0 * math.pi / total * phase.astype(jnp.float32)
    return (cos_outer, sin_outer, cos_inner, sin_inner, jnp.cos(angle), jnp.sin(angle))


def forward_dft(signal, tables):
    cos_outer, sin_outer, cos_inner, sin_inner, turn_cos, turn_sin = tables
    blocks = signal.shape[0]
    real_part = jnp.einsum("kn,ncb->ckb", cos_outer[:, :blocks], signal, precision=HIGHEST)
    imag_part = -jnp.einsum("kn,ncb->ckb", sin_outer[:, :blocks], signal, precision=HIGHEST)
    twisted_real = real_part * turn_cos + imag_part * turn_sin
    twisted_imag = imag_part * turn_cos - real_part * turn_sin
    spec_real = jnp.einsum("ckn,nm->ckm", twisted_real, cos_inner, precision=HIGHEST) + jnp.einsum(
        "ckn,nm->ckm", twisted_imag, sin_inner, precision=HIGHEST
    )
    spec_imag = jnp.einsum("ckn,nm->ckm", twisted_imag, cos_inner, precision=HIGHEST) - jnp.einsum(
        "ckn,nm->ckm", twisted_real, sin_inner, precision=HIGHEST
    )
    return (spec_real, spec_imag)


def inverse_dft(spec_real, spec_imag, tables, blocks):
    cos_outer, sin_outer, cos_inner, sin_inner, turn_cos, turn_sin = tables
    total = cos_outer.shape[0] * cos_inner.shape[0]
    inner_real = jnp.einsum("ckm,mn->ckn", spec_real, cos_inner, precision=HIGHEST) - jnp.einsum(
        "ckm,mn->ckn", spec_imag, sin_inner, precision=HIGHEST
    )
    inner_imag = jnp.einsum("ckm,mn->ckn", spec_real, sin_inner, precision=HIGHEST) + jnp.einsum(
        "ckm,mn->ckn", spec_imag, cos_inner, precision=HIGHEST
    )
    turned_real = inner_real * turn_cos - inner_imag * turn_sin
    turned_imag = inner_real * turn_sin + inner_imag * turn_cos
    result = jnp.einsum(
        "nk,ckb->ncb", cos_outer[:blocks, :], turned_real, precision=HIGHEST
    ) - jnp.einsum("nk,ckb->ncb", sin_outer[:blocks, :], turned_imag, precision=HIGHEST)
    return result / total


def causal_conv(sent_value, filter_spec, tables):
    value_real, value_imag = forward_dft(sent_value.astype(jnp.float32), tables)
    filter_real, filter_imag = filter_spec
    product_real = value_real * filter_real - value_imag * filter_imag
    product_imag = value_real * filter_imag + value_imag * filter_real
    return inverse_dft(product_real, product_imag, tables, sent_value.shape[0]).astype(jnp.bfloat16)


def transposed_conv(sent_grad, filter_spec, tables):
    grad_real, grad_imag = forward_dft(sent_grad.astype(jnp.float32), tables)
    filter_real, filter_imag = filter_spec
    product_real = grad_real * filter_real + grad_imag * filter_imag
    product_imag = grad_imag * filter_real - grad_real * filter_imag
    return inverse_dft(product_real, product_imag, tables, sent_grad.shape[0]).astype(jnp.bfloat16)


def split_body(value, gate, long_filter, skip_gain, cotangent, owner_map):
    blocks = lax.axis_size("seq")
    tok_rows = value.shape[0]
    group = value.shape[1]
    per_device = group // blocks
    value_rows = value.astype(jnp.float32)
    gate_rows = gate.astype(jnp.float32)
    grad_rows = (cotangent.astype(jnp.float32) * gate_rows).astype(jnp.bfloat16)
    value_major = value.T
    grad_major = grad_rows.T
    tables = make_tables(2 * blocks, tok_rows)
    value_split = value_major.reshape(blocks, per_device, tok_rows)
    filter_split = long_filter.reshape(blocks, per_device, tok_rows)
    grad_split = grad_major.reshape(blocks, per_device, tok_rows)
    sent_value, sent_filter = (
        lax.all_to_all(value_split, "seq", split_axis=0, concat_axis=0, tiled=True),
        lax.all_to_all(filter_split, "seq", split_axis=0, concat_axis=0, tiled=True),
    )
    filter_spec = forward_dft(sent_filter.astype(jnp.float32), tables)
    conv_back = lax.all_to_all(
        causal_conv(sent_value, filter_spec, tables), "seq", split_axis=0, concat_axis=0, tiled=True
    )
    sent_grad = lax.all_to_all(grad_split, "seq", split_axis=0, concat_axis=0, tiled=True)
    grad_back = lax.all_to_all(
        transposed_conv(sent_grad, filter_spec, tables),
        "seq",
        split_axis=0,
        concat_axis=0,
        tiled=True,
    )
    conv_rows = conv_back.reshape(group, tok_rows).T.astype(jnp.float32)
    mixed = conv_rows + skip_gain * value_rows
    output = (gate_rows * mixed).astype(jnp.bfloat16)
    gate_grad = (cotangent.astype(jnp.float32) * mixed).astype(jnp.bfloat16)
    back_rows = grad_back.reshape(group, tok_rows).T.astype(jnp.float32)
    grad_float = grad_rows.astype(jnp.float32)
    value_grad = (back_rows + skip_gain * grad_float).astype(jnp.bfloat16)
    scale = 1.0 / math.sqrt(tok_rows * blocks)
    local_sums = (
        jnp.sum(sent_value.astype(jnp.float32) * sent_grad.astype(jnp.float32), axis=(0, 2)) * scale
    )
    gathered = lax.all_gather(local_sums.reshape(1, per_device), "seq", axis=0, tiled=True)
    mine = owner_map[lax.axis_index("seq")]
    summed = lax.dynamic_slice_in_dim(gathered, mine, 1, 0)
    gain_grad = summed.reshape(1, 1, per_device)
    return (output, value_grad, gate_grad, gain_grad)


LANES = 128
DEVICE_VMEM = 67043328
FILTER, VALUE, GRAD, CONV, BACK, SUMS = range(6)
MESH = pl.DeviceIdType.MESH


def block_tables(rows):
    angle = math.pi / (2 * rows) * (2 * np.arange(rows, dtype=np.float64)[:, None] + 1)
    tokens = angle * np.arange(rows, dtype=np.float64)[None, :]
    window = angle * np.arange(-rows, rows, dtype=np.float64)[None, :]

    def parts(wide):
        high = wide.astype(jnp.bfloat16)
        return high, (wide - high.astype(np.float64)).astype(jnp.bfloat16)

    signal_high, signal_low = parts(np.concatenate([np.cos(tokens), -np.sin(tokens)]))
    window_high, window_low = parts(np.concatenate([np.cos(window), -np.sin(window)]))
    back = np.concatenate([np.cos(tokens), -np.sin(tokens)]).T / rows
    back_high, back_low = parts(back)
    return (
        np.concatenate([signal_high, signal_low], axis=1),
        np.concatenate([window_high, window_low], axis=1),
        np.concatenate([back_high, back_low, back_high], axis=1),
    )


def fused_kernel(
    n,
    value,
    filt,
    gate,
    cot,
    skip,
    owner,
    signal_any,
    window_any,
    back_any,
    output,
    value_grad,
    gate_grad,
    gain,
    signal_table,
    window_table,
    back_table,
    value_loc,
    gate_loc,
    cot_loc,
    grad_loc,
    seq_value,
    seq_filter,
    taps,
    seq_grad,
    spec_value,
    spec_filter,
    spec_grad,
    product,
    conv_out,
    back_out,
    conv_in,
    back_in,
    sums_out,
    sums_in,
    send_sem,
    recv_sem,
    local_sem,
):
    me = lax.axis_index("seq")
    rows, group = value.shape
    chans = group // n
    length = rows * n
    offsets = sorted(range(1, n), key=lambda i: abs(2 * i - n))

    def peer_of(offset):
        return lax.rem(me + offset, n)

    def cols(index):
        return pl.ds(pl.multiple_of(index * chans, chans), chans)

    def copy_of(kind, peer, sender):
        if kind == FILTER:
            pair = filt.at[cols(peer), :], seq_filter.at[sender]
        elif kind == VALUE:
            pair = value.at[:, cols(peer)], seq_value.at[sender]
        elif kind == GRAD:
            pair = grad_loc.at[:, cols(peer)], seq_grad.at[sender]
        elif kind == CONV:
            pair = conv_out.at[peer], conv_in.at[sender]
        elif kind == BACK:
            pair = back_out.at[peer], back_in.at[sender]
        else:
            pair = sums_out, sums_in.at[sender]
        return pltpu.make_async_remote_copy(
            src_ref=pair[0],
            dst_ref=pair[1],
            send_sem=send_sem.at[kind, peer],
            recv_sem=recv_sem.at[kind, sender],
            device_id={"seq": peer},
            device_id_type=MESH,
        )

    def send(kind):
        for offset in offsets:
            peer = peer_of(offset)
            copy_of(kind, peer, me).start()

    def receive(kind):
        for offset in reversed(offsets):
            peer = peer_of(offset)
            copy_of(kind, peer, peer).wait_recv()

    barrier = pltpu.get_barrier_semaphore()
    for offset in offsets:
        pl.semaphore_signal(barrier, inc=1, device_id={"seq": peer_of(offset)}, device_id_type=MESH)
    local = [
        pltpu.make_async_copy(gate, gate_loc, local_sem.at[0]),
        pltpu.make_async_copy(cot, cot_loc, local_sem.at[1]),
        pltpu.make_async_copy(value, value_loc, local_sem.at[2]),
        pltpu.make_async_copy(filt.at[cols(me), :], seq_filter.at[me], local_sem.at[3]),
        pltpu.make_async_copy(value.at[:, cols(me)], seq_value.at[me], local_sem.at[4]),
        pltpu.make_async_copy(signal_any, signal_table, local_sem.at[5]),
        pltpu.make_async_copy(window_any, window_table, local_sem.at[6]),
        pltpu.make_async_copy(back_any, back_table, local_sem.at[7]),
    ]
    for copy in local:
        copy.start()
    local[0].wait()
    local[1].wait()
    grad_loc[...] = (cot_loc[...].astype(jnp.float32) * gate_loc[...].astype(jnp.float32)).astype(
        jnp.bfloat16
    )
    seq_grad[me] = grad_loc[:, cols(me)]
    pl.semaphore_wait(barrier, n - 1)
    for kind in (FILTER, VALUE, GRAD):
        send(kind)
    for copy in local[2:]:
        copy.wait()

    def dot(left, right):
        return jnp.dot(left, right, preferred_element_type=jnp.float32)

    def spectrum(signal, result):
        for index in range(0, n, 2):
            pair = jnp.concatenate([signal[index], signal[index + 1]], axis=1)
            both = dot(signal_table[...], jnp.concatenate([pair, pair], axis=0))
            result[index] = both[:, :chans]
            result[index + 1] = both[:, chans:]

    def multiply(left, pairs):
        @pl.loop(0, rows // 8)
        def _(step):
            real = pl.ds(pl.multiple_of(step * 8, 8), 8)
            imag = pl.ds(pl.multiple_of(rows + step * 8, 8), 8)
            left_real = [left[c, real, :] for c in range(n)]
            left_imag = [left[c, imag, :] for c in range(n)]
            for index in range(n):
                total_real = total_imag = None
                for c, d, sign in pairs(index):
                    with_real = spec_filter[d, real, :]
                    with_imag = spec_filter[d, imag, :]
                    one, two = left_real[c] * with_real, left_imag[c] * with_imag
                    three, four = left_imag[c] * with_real, left_real[c] * with_imag
                    term_real, term_imag = (
                        (one - two, three + four) if sign > 0 else (one + two, three - four)
                    )
                    total_real = term_real if total_real is None else total_real + term_real
                    total_imag = term_imag if total_imag is None else total_imag + term_imag
                product[index, real, :] = total_real
                product[index, imag, :] = total_imag

    def inverse(result):
        for index in range(0, n, 2):
            wide = jnp.concatenate([product[index], product[index + 1]], axis=1)
            high = wide.astype(jnp.bfloat16)
            low = (wide - high.astype(jnp.float32)).astype(jnp.bfloat16)
            both = dot(back_table[...], jnp.concatenate([high, high, low], axis=0))
            result[index] = both[:, :chans].astype(jnp.bfloat16)
            result[index + 1] = both[:, chans:].astype(jnp.bfloat16)

    receive(FILTER)
    for index in range(n):
        taps[(index + 1) * rows : (index + 2) * rows, :] = (
            seq_filter[index].astype(jnp.float32).T.astype(jnp.bfloat16)
        )
    taps[:rows, :] = jnp.zeros((rows, chans), jnp.bfloat16)
    for index in range(0, n, 2):
        pair = jnp.concatenate(
            [
                taps[index * rows : (index + 2) * rows, :],
                taps[(index + 1) * rows : (index + 3) * rows, :],
            ],
            axis=1,
        )
        both = dot(window_table[...], jnp.concatenate([pair, pair], axis=0))
        spec_filter[index] = both[:, :chans]
        spec_filter[index + 1] = both[:, chans:]

    receive(VALUE)
    spectrum(seq_value, spec_value)
    multiply(spec_value, lambda b: [(c, b - c, 1) for c in range(b + 1)])
    inverse(conv_out)
    send(CONV)

    receive(GRAD)
    spectrum(seq_grad, spec_grad)
    multiply(spec_grad, lambda b: [(c, c - b, -1) for c in range(b, n)])
    inverse(back_out)
    send(BACK)

    total = jnp.zeros((rows, chans), jnp.float32)
    for index in range(n):
        total = total + seq_value[index].astype(jnp.float32) * seq_grad[index].astype(jnp.float32)
    sums = jnp.sum(total, axis=0, keepdims=True) * (1.0 / math.sqrt(length))
    sums_out[...] = jnp.broadcast_to(sums, sums_out.shape)
    sums_in[me] = jnp.broadcast_to(sums, sums_out.shape)
    send(SUMS)

    def finish_conv(index, conv):
        at = cols(index)
        cot_rows = cot_loc[:, at].astype(jnp.float32)
        gate_rows = gate_loc[:, at].astype(jnp.float32)
        mixed = conv.astype(jnp.float32) + skip[:, at] * value_loc[:, at].astype(jnp.float32)
        output[:, at] = (gate_rows * mixed).astype(jnp.bfloat16)
        gate_grad[:, at] = (cot_rows * mixed).astype(jnp.bfloat16)

    def finish_back(index, back):
        at = cols(index)
        grads = grad_loc[:, at].astype(jnp.float32)
        value_grad[:, at] = (back.astype(jnp.float32) + skip[:, at] * grads).astype(jnp.bfloat16)

    finish_conv(me, conv_out[me])
    finish_back(me, back_out[me])
    for kind, finish, landed in ((CONV, finish_conv, conv_in), (BACK, finish_back, back_in)):
        for offset in reversed(offsets):
            peer = peer_of(offset)
            copy_of(kind, peer, peer).wait_recv()
            finish(peer, landed[peer])
    receive(SUMS)
    gain[...] = sums_in[owner[me]][:1, :]
    for kind in range(6):
        for offset in offsets:
            peer = peer_of(offset)
            copy_of(kind, peer, me).wait_send()


def finish_kernel(
    output_loc, value_grad_loc, gate_grad_loc, gain_loc, output, value_grad, gate_grad, gain, sem
):
    copies = [
        pltpu.make_async_copy(source, target, sem.at[index])
        for index, (source, target) in enumerate(
            (
                (output_loc, output),
                (value_grad_loc, value_grad),
                (gate_grad_loc, gate_grad),
                (gain_loc, gain),
            )
        )
    ]
    for copy in copies:
        copy.start()
    for copy in copies:
        copy.wait()


def fused_body(value, gate, long_filter, skip_gain, cotangent, owner_map):
    n = lax.axis_size("seq")
    rows, group = value.shape
    chans = group // n
    tables = block_tables(rows)
    anywhere = pl.BlockSpec(memory_space=pltpu.HBM)
    vmem = pl.BlockSpec(memory_space=pltpu.VMEM)
    bf16, f32 = jnp.bfloat16, jnp.float32
    spec = pltpu.VMEM((n, 2 * rows, chans), f32)
    tokens = pltpu.VMEM((rows, group), bf16)
    blocks = pltpu.VMEM((n, rows, chans), bf16)
    local = pl.pallas_call(
        functools.partial(fused_kernel, n),
        out_shape=(tokens, tokens, tokens, pltpu.VMEM((1, chans), f32)),
        in_specs=[
            anywhere,
            anywhere,
            anywhere,
            anywhere,
            vmem,
            pl.BlockSpec(memory_space=pltpu.SMEM),
            anywhere,
            anywhere,
            anywhere,
        ],
        out_specs=(vmem,) * 4,
        scratch_shapes=[
            *(pltpu.VMEM(table.shape, bf16) for table in tables),
            tokens,
            tokens,
            tokens,
            tokens,
            blocks,
            pltpu.VMEM((n, chans, rows), bf16),
            pltpu.VMEM(((n + 1) * rows, chans), bf16),
            blocks,
            spec,
            spec,
            spec,
            spec,
            blocks,
            blocks,
            blocks,
            blocks,
            pltpu.VMEM((8, chans), f32),
            pltpu.VMEM((n, 8, chans), f32),
            pltpu.SemaphoreType.DMA((6, n)),
            pltpu.SemaphoreType.DMA((6, n)),
            pltpu.SemaphoreType.DMA((8,)),
        ],
        compiler_params=pltpu.CompilerParams(
            collective_id=0,
            has_side_effects=True,
            vmem_limit_bytes=DEVICE_VMEM - 6 * rows * group - 2**16,
        ),
    )(
        value,
        long_filter,
        gate,
        cotangent,
        skip_gain.reshape(1, group),
        owner_map,
        *tables,
    )
    result = jax.ShapeDtypeStruct((rows, group), bf16)
    output, value_grad, gate_grad, gain = pl.pallas_call(
        finish_kernel,
        out_shape=(result, result, result, jax.ShapeDtypeStruct((1, chans), f32)),
        in_specs=[vmem] * 4,
        out_specs=(anywhere,) * 4,
        scratch_shapes=[pltpu.SemaphoreType.DMA((4,))],
        compiler_params=pltpu.CompilerParams(vmem_limit_bytes=2**20),
    )(*local)
    return (output, value_grad, gate_grad, gain.reshape(1, 1, chans))


def body(value, gate, long_filter, skip_gain, cotangent, owner_map):
    n = lax.axis_size("seq")
    rows, group = value.shape
    aligned = rows % LANES == 0 and group % (n * LANES) == 0 and n % 2 == 0
    needed = 64 * rows * group + 48 * rows * rows
    chosen = fused_body if aligned and needed <= DEVICE_VMEM // 2 else split_body
    return chosen(value, gate, long_filter, skip_gain, cotangent, owner_map)


def solution(mesh):
    in_specs = (
        P("seq", "chan"),
        P("seq", "chan"),
        P("chan", "seq"),
        P("chan"),
        P("seq", "chan"),
        P(),
    )
    out_specs = (P("seq", "chan"), P("seq", "chan"), P("seq", "chan"), P("chan", "seq", None))
    return jax.shard_map(body, mesh=mesh, in_specs=in_specs, out_specs=out_specs, check_vma=False)
```

```python
import functools
import math

import jax
import jax.numpy as jnp
import numpy as np
from jax import lax
from jax.experimental import pallas as pl
from jax.experimental.pallas import tpu as pltpu
from jax.sharding import PartitionSpec as P

HIGHEST = lax.Precision.HIGHEST


def dft_table(size):
    index = jnp.arange(size, dtype=jnp.int32)
    phase = index[:, None] * index[None, :] % size
    angle = 2.0 * math.pi / size * phase.astype(jnp.float32)
    return (jnp.cos(angle), jnp.sin(angle))


def make_tables(outer, inner):
    cos_outer, sin_outer = dft_table(outer)
    cos_inner, sin_inner = dft_table(inner)
    total = outer * inner
    phase = (
        jnp.arange(outer, dtype=jnp.int32)[:, None]
        * jnp.arange(inner, dtype=jnp.int32)[None, :]
        % total
    )
    angle = 2.0 * math.pi / total * phase.astype(jnp.float32)
    return (cos_outer, sin_outer, cos_inner, sin_inner, jnp.cos(angle), jnp.sin(angle))


def forward_dft(signal, tables):
    cos_outer, sin_outer, cos_inner, sin_inner, turn_cos, turn_sin = tables
    blocks = signal.shape[0]
    real_part = jnp.einsum("kn,ncb->ckb", cos_outer[:, :blocks], signal, precision=HIGHEST)
    imag_part = -jnp.einsum("kn,ncb->ckb", sin_outer[:, :blocks], signal, precision=HIGHEST)
    twisted_real = real_part * turn_cos + imag_part * turn_sin
    twisted_imag = imag_part * turn_cos - real_part * turn_sin
    spec_real = jnp.einsum("ckn,nm->ckm", twisted_real, cos_inner, precision=HIGHEST) + jnp.einsum(
        "ckn,nm->ckm", twisted_imag, sin_inner, precision=HIGHEST
    )
    spec_imag = jnp.einsum("ckn,nm->ckm", twisted_imag, cos_inner, precision=HIGHEST) - jnp.einsum(
        "ckn,nm->ckm", twisted_real, sin_inner, precision=HIGHEST
    )
    return (spec_real, spec_imag)


def inverse_dft(spec_real, spec_imag, tables, blocks):
    cos_outer, sin_outer, cos_inner, sin_inner, turn_cos, turn_sin = tables
    total = cos_outer.shape[0] * cos_inner.shape[0]
    inner_real = jnp.einsum("ckm,mn->ckn", spec_real, cos_inner, precision=HIGHEST) - jnp.einsum(
        "ckm,mn->ckn", spec_imag, sin_inner, precision=HIGHEST
    )
    inner_imag = jnp.einsum("ckm,mn->ckn", spec_real, sin_inner, precision=HIGHEST) + jnp.einsum(
        "ckm,mn->ckn", spec_imag, cos_inner, precision=HIGHEST
    )
    turned_real = inner_real * turn_cos - inner_imag * turn_sin
    turned_imag = inner_real * turn_sin + inner_imag * turn_cos
    result = jnp.einsum(
        "nk,ckb->ncb", cos_outer[:blocks, :], turned_real, precision=HIGHEST
    ) - jnp.einsum("nk,ckb->ncb", sin_outer[:blocks, :], turned_imag, precision=HIGHEST)
    return result / total


def causal_conv(sent_value, filter_spec, tables):
    value_real, value_imag = forward_dft(sent_value.astype(jnp.float32), tables)
    filter_real, filter_imag = filter_spec
    product_real = value_real * filter_real - value_imag * filter_imag
    product_imag = value_real * filter_imag + value_imag * filter_real
    return inverse_dft(product_real, product_imag, tables, sent_value.shape[0]).astype(jnp.bfloat16)


def transposed_conv(sent_grad, filter_spec, tables):
    grad_real, grad_imag = forward_dft(sent_grad.astype(jnp.float32), tables)
    filter_real, filter_imag = filter_spec
    product_real = grad_real * filter_real + grad_imag * filter_imag
    product_imag = grad_imag * filter_real - grad_real * filter_imag
    return inverse_dft(product_real, product_imag, tables, sent_grad.shape[0]).astype(jnp.bfloat16)


def split_body(value, gate, long_filter, skip_gain, cotangent, owner_map):
    blocks = lax.axis_size("seq")
    tok_rows = value.shape[0]
    group = value.shape[1]
    per_device = group // blocks
    value_rows = value.astype(jnp.float32)
    gate_rows = gate.astype(jnp.float32)
    grad_rows = (cotangent.astype(jnp.float32) * gate_rows).astype(jnp.bfloat16)
    value_major = value.T
    grad_major = grad_rows.T
    tables = make_tables(2 * blocks, tok_rows)
    value_split = value_major.reshape(blocks, per_device, tok_rows)
    filter_split = long_filter.reshape(blocks, per_device, tok_rows)
    grad_split = grad_major.reshape(blocks, per_device, tok_rows)
    sent_value, sent_filter = (
        lax.all_to_all(value_split, "seq", split_axis=0, concat_axis=0, tiled=True),
        lax.all_to_all(filter_split, "seq", split_axis=0, concat_axis=0, tiled=True),
    )
    filter_spec = forward_dft(sent_filter.astype(jnp.float32), tables)
    conv_back = lax.all_to_all(
        causal_conv(sent_value, filter_spec, tables), "seq", split_axis=0, concat_axis=0, tiled=True
    )
    sent_grad = lax.all_to_all(grad_split, "seq", split_axis=0, concat_axis=0, tiled=True)
    grad_back = lax.all_to_all(
        transposed_conv(sent_grad, filter_spec, tables),
        "seq",
        split_axis=0,
        concat_axis=0,
        tiled=True,
    )
    conv_rows = conv_back.reshape(group, tok_rows).T.astype(jnp.float32)
    mixed = conv_rows + skip_gain * value_rows
    output = (gate_rows * mixed).astype(jnp.bfloat16)
    gate_grad = (cotangent.astype(jnp.float32) * mixed).astype(jnp.bfloat16)
    back_rows = grad_back.reshape(group, tok_rows).T.astype(jnp.float32)
    grad_float = grad_rows.astype(jnp.float32)
    value_grad = (back_rows + skip_gain * grad_float).astype(jnp.bfloat16)
    scale = 1.0 / math.sqrt(tok_rows * blocks)
    local_sums = (
        jnp.sum(sent_value.astype(jnp.float32) * sent_grad.astype(jnp.float32), axis=(0, 2)) * scale
    )
    gathered = lax.all_gather(local_sums.reshape(1, per_device), "seq", axis=0, tiled=True)
    mine = owner_map[lax.axis_index("seq")]
    summed = lax.dynamic_slice_in_dim(gathered, mine, 1, 0)
    gain_grad = summed.reshape(1, 1, per_device)
    return (output, value_grad, gate_grad, gain_grad)


LANES = 128
DEVICE_VMEM = 67043328
FILTER, NARROW, WIDE_NEAR, WIDE_FAR, RESULT_NARROW, RESULT_WIDE, KINDS = range(7)
MESH = pl.DeviceIdType.MESH


def block_tables(rows):
    angle = math.pi / (2 * rows) * (2 * np.arange(rows, dtype=np.float64)[:, None] + 1)
    tokens = angle * np.arange(rows, dtype=np.float64)[None, :]
    window = angle * np.arange(-rows, rows, dtype=np.float64)[None, :]

    def parts(wide):
        high = wide.astype(jnp.bfloat16)
        return high, (wide - high.astype(np.float64)).astype(jnp.bfloat16)

    signal_high, signal_low = parts(np.concatenate([np.cos(tokens), -np.sin(tokens)]))
    window_high, window_low = parts(np.concatenate([np.cos(window), -np.sin(window)]))
    back = np.concatenate([np.cos(tokens), -np.sin(tokens)]).T / rows
    back_high, back_low = parts(back)
    return (
        np.concatenate([signal_high, signal_low], axis=1),
        np.concatenate([window_high, window_low], axis=1),
        np.concatenate([back_high, back_low, back_high], axis=1),
    )


def fused_kernel(
    n,
    value,
    filt,
    gate,
    cot,
    skip_any,
    owner_any,
    signal_any,
    window_any,
    back_any,
    output,
    value_grad,
    gate_grad,
    gain,
    signal_table,
    window_table,
    back_table,
    skip,
    owner,
    value_loc,
    gate_loc,
    cot_loc,
    grad_loc,
    filter_in,
    narrow_in,
    wide_in,
    taps,
    spec_filter,
    spec_signal,
    product_narrow,
    product_wide,
    narrow_out,
    wide_out,
    conv_in,
    back_in,
    sums_out,
    sums_in,
    sums_table,
    send_sem,
    recv_sem,
    result_sem,
    sums_send_sem,
    sums_sem,
    local_sem,
):
    me = lax.axis_index("seq")
    half = n // 2
    rows, group = value.shape
    chans = group // n
    length = rows * n
    lower = me < half
    mirror = n - 1 - me
    mine = lax.rem(me, half)
    place = jnp.where(lower, me, mirror)
    near_first = jnp.where(lower, 0, half)

    def cols(index, tile):
        return pl.ds(pl.multiple_of((2 * index + tile) * chans, chans), chans)

    def other(device, action):
        @pl.when(device != me)
        def _():
            action()

    def start(source, target, device, sent, arrival):
        def action():
            pltpu.make_async_remote_copy(
                src_ref=source,
                dst_ref=target,
                send_sem=sent,
                recv_sem=arrival,
                device_id={"seq": device},
                device_id_type=MESH,
            ).start()

        other(device, action)

    def wait_for(semaphore, blocks):
        pltpu.make_async_copy(blocks, blocks, semaphore).wait()

    barrier = pltpu.get_barrier_semaphore()

    @pl.loop(0, n)
    def _(device):
        def greet():
            pl.semaphore_signal(barrier, inc=1, device_id={"seq": device}, device_id_type=MESH)

        other(device, greet)

    local = [
        pltpu.make_async_copy(gate, gate_loc, local_sem.at[0]),
        pltpu.make_async_copy(cot, cot_loc, local_sem.at[1]),
        pltpu.make_async_copy(value, value_loc, local_sem.at[2]),
        pltpu.make_async_copy(signal_any, signal_table, local_sem.at[3]),
        pltpu.make_async_copy(window_any, window_table, local_sem.at[4]),
        pltpu.make_async_copy(back_any, back_table, local_sem.at[5]),
        pltpu.make_async_copy(skip_any, skip, local_sem.at[6]),
        pltpu.make_async_copy(owner_any, owner, local_sem.at[7]),
        pltpu.make_async_copy(filt.at[cols(mine, 0), :], filter_in.at[0, me], local_sem.at[8]),
        pltpu.make_async_copy(filt.at[cols(mine, 1), :], filter_in.at[1, me], local_sem.at[9]),
    ]
    for copy in local:
        copy.start()
    pl.semaphore_wait(barrier, n - 1)

    def send(kind, source_of, target, tile, far):
        first = half - near_first if far else near_first

        @pl.loop(0, half)
        def _(step):
            index = lax.rem(mine + 1 + step, half)
            start(
                source_of(index),
                target,
                first + index,
                send_sem.at[kind, tile],
                recv_sem.at[kind, tile],
            )

    def send_filter(tile, far):
        send(FILTER, lambda i: filt.at[cols(i, tile), :], filter_in.at[tile, me], tile, far)

    def send_value(tile, far, near):
        def source(index):
            return value.at[:, cols(index, tile)]

        @pl.when(lower)
        def _():
            if far:
                send(WIDE_FAR, source, wide_in.at[tile, me], tile, True)
            if near:
                send(NARROW, source, narrow_in.at[tile, me], tile, False)

        if near:

            @pl.when(jnp.logical_not(lower))
            def _():
                send(WIDE_NEAR, source, wide_in.at[tile, me], tile, False)

    def send_grad(tile, far, near):
        def source(index):
            return grad_loc.at[:, cols(index, tile)]

        @pl.when(jnp.logical_not(lower))
        def _():
            if far:
                send(WIDE_FAR, source, wide_in.at[tile, mirror], tile, True)
            if near:
                send(NARROW, source, narrow_in.at[tile, mirror], tile, False)

        if near:

            @pl.when(lower)
            def _():
                send(WIDE_NEAR, source, wide_in.at[tile, mirror], tile, False)

    def make_grads():
        local[0].wait()
        local[1].wait()

        @pl.loop(0, rows // 16)
        def _(step):
            at = pl.ds(pl.multiple_of(step * 16, 16), 16)
            grads = cot_loc[at, :].astype(jnp.float32) * gate_loc[at, :].astype(jnp.float32)
            grad_loc[at, :] = grads.astype(jnp.bfloat16)

    @pl.loop(0, 2)
    def _(tile):
        send_filter(tile, True)
        send_filter(tile, False)

    make_grads()

    @pl.loop(0, 2)
    def _(tile):
        send_value(tile, False, True)
        send_grad(tile, False, True)

    @pl.loop(0, 2)
    def _(tile):
        send_value(tile, True, False)
        send_grad(tile, True, False)
    for copy in local[2:]:
        copy.wait()

    def dot(left, right):
        return jnp.dot(left, right, preferred_element_type=jnp.float32)

    def spectrum(signal, tile, first):
        @pl.loop(0, half, step=2, unroll=True)
        def _(block):
            pair = jnp.concatenate(
                [signal[tile, first + block], signal[tile, first + block + 1]], axis=1
            )
            both = dot(signal_table[...], jnp.concatenate([pair, pair], axis=0))
            spec_signal[block] = both[:, :chans]
            spec_signal[block + 1] = both[:, chans:]

    def multiply(result, tile, sign, pairs, windows, adds):
        @pl.loop(0, rows // 8)
        def _(step):
            real = pl.ds(pl.multiple_of(step * 8, 8), 8)
            imag = pl.ds(pl.multiple_of(rows + step * 8, 8), 8)
            signal_real = [spec_signal[c, real, :] for c in range(half)]
            signal_imag = [spec_signal[c, imag, :] for c in range(half)]
            filter_real = {d: spec_filter[tile, d, real, :] for d in windows}
            filter_imag = {d: spec_filter[tile, d, imag, :] * sign for d in windows}
            for block in range(half):
                total_real = result[tile, block, real, :] if adds else None
                total_imag = result[tile, block, imag, :] if adds else None
                for c, d in pairs(block):
                    with_real, with_imag = filter_real[d], filter_imag[d]
                    term_real = signal_real[c] * with_real - signal_imag[c] * with_imag
                    term_imag = signal_imag[c] * with_real + signal_real[c] * with_imag
                    total_real = term_real if total_real is None else total_real + term_real
                    total_imag = term_imag if total_imag is None else total_imag + term_imag
                result[tile, block, real, :] = total_real
                result[tile, block, imag, :] = total_imag

    def multiply_near(result, tile, sign):
        multiply(
            result, tile, sign, lambda b: [(c, b - c) for c in range(b + 1)], range(half), False
        )

    def multiply_far(result, tile, sign):
        multiply(
            result,
            tile,
            sign,
            lambda b: [(c, half + b - c) for c in range(half)],
            range(1, n),
            True,
        )

    def inverse(product, result, tile):
        @pl.loop(0, half, step=2, unroll=True)
        def _(block):
            wide = jnp.concatenate([product[tile, block], product[tile, block + 1]], axis=1)
            high = wide.astype(jnp.bfloat16)
            low = (wide - high.astype(jnp.float32)).astype(jnp.bfloat16)
            both = dot(back_table[...], jnp.concatenate([high, high, low], axis=0))
            result[tile, block] = both[:, :chans].astype(jnp.bfloat16)
            result[tile, block + 1] = both[:, chans:].astype(jnp.bfloat16)

    def filter_spectra(tile):
        wait_for(recv_sem.at[FILTER, tile], filter_in.at[tile, pl.ds(0, n - 1)])
        taps[0] = jnp.zeros(taps.shape[1:], jnp.bfloat16)

        @pl.loop(0, n, unroll=True)
        def _(block):
            taps[block + 1] = filter_in[tile, block].astype(jnp.float32).T.astype(jnp.bfloat16)

        @pl.loop(0, n, step=2, unroll=True)
        def _(block):
            before, here, after = taps[block], taps[block + 1], taps[block + 2]
            pair = jnp.concatenate(
                [
                    jnp.concatenate([before, here], axis=0),
                    jnp.concatenate([here, after], axis=0),
                ],
                axis=1,
            )
            both = dot(window_table[...], jnp.concatenate([pair, pair], axis=0))
            spec_filter[tile, block] = both[:, :chans]
            spec_filter[tile, block + 1] = both[:, chans:]

    def send_results(kind, source_of, target, slot, tile):
        @pl.loop(0, half)
        def _(step):
            index = lax.rem(mine + 1 + step, half)
            start(
                source_of(index),
                target.at[:, cols(mine, tile)],
                near_first + index,
                send_sem.at[kind, tile],
                result_sem.at[slot, tile, mine],
            )

        target[:, cols(mine, tile)] = source_of(mine)[...]

    def narrow_results(tile):
        @pl.when(lower)
        def _():
            narrow_in[tile, place] = value_loc[:, cols(mine, tile)]

        @pl.when(jnp.logical_not(lower))
        def _():
            narrow_in[tile, place] = grad_loc[:, cols(mine, tile)]

        wait_for(recv_sem.at[NARROW, tile], narrow_in.at[tile, pl.ds(0, half - 1)])
        spectrum(narrow_in, tile, 0)
        multiply_near(product_narrow, tile, jnp.where(lower, 1.0, -1.0))
        inverse(product_narrow, narrow_out, tile)

        @pl.when(lower)
        def _():
            send_results(RESULT_NARROW, lambda index: narrow_out.at[tile, index], conv_in, 0, tile)

        @pl.when(jnp.logical_not(lower))
        def _():
            send_results(RESULT_NARROW, lambda index: narrow_out.at[tile, half - 1 - index], back_in, 1, tile)

    def wide_near(tile):
        @pl.when(lower)
        def _():
            wide_in[tile, mirror] = grad_loc[:, cols(mine, tile)]

        @pl.when(jnp.logical_not(lower))
        def _():
            wide_in[tile, me] = value_loc[:, cols(mine, tile)]

        wait_for(recv_sem.at[WIDE_NEAR, tile], wide_in.at[tile, pl.ds(0, half - 1)])
        tile_sums(tile)
        spectrum(wide_in, tile, half)
        multiply_near(product_wide, tile, jnp.where(lower, -1.0, 1.0))

    def wide_results(tile):
        wait_for(recv_sem.at[WIDE_FAR, tile], wide_in.at[tile, pl.ds(0, half)])
        spectrum(wide_in, tile, 0)
        multiply_far(product_wide, tile, jnp.where(lower, -1.0, 1.0))
        inverse(product_wide, wide_out, tile)

        @pl.when(lower)
        def _():
            send_results(RESULT_WIDE, lambda index: wide_out.at[tile, half - 1 - index], back_in, 1, tile)

        @pl.when(jnp.logical_not(lower))
        def _():
            send_results(RESULT_WIDE, lambda index: wide_out.at[tile, index], conv_in, 0, tile)

    def tile_sums(tile):
        @pl.loop(0, rows // 16, init_carry=jnp.zeros((16, chans), jnp.float32))
        def total(step, carry):
            at = pl.ds(pl.multiple_of(step * 16, 16), 16)
            for block in range(half):
                carry += narrow_in[tile, block, at, :].astype(jnp.float32) * wide_in[
                    tile, n - 1 - block, at, :
                ].astype(jnp.float32)
            return carry

        sums_out[tile] = jnp.sum(total, axis=0, keepdims=True) * (1.0 / math.sqrt(length))
        sums_in[me, tile] = sums_out[tile]

        @pl.loop(0, n)
        def _(device):
            start(
                sums_out.at[tile],
                sums_in.at[me, tile],
                device,
                sums_send_sem.at[tile],
                sums_sem.at[me, tile],
            )

    for stage in (filter_spectra, narrow_results, wide_near, wide_results):
        pl.loop(0, 2)(stage)

    def finish_conv(at):
        cot_rows = cot_loc[:, at].astype(jnp.float32)
        gate_rows = gate_loc[:, at].astype(jnp.float32)
        mixed = conv_in[:, at].astype(jnp.float32) + skip[:, at] * value_loc[:, at].astype(
            jnp.float32
        )
        output[:, at] = (gate_rows * mixed).astype(jnp.bfloat16)
        gate_grad[:, at] = (cot_rows * mixed).astype(jnp.bfloat16)

    def finish_back(at):
        grads = grad_loc[:, at].astype(jnp.float32)
        value_grad[:, at] = (back_in[:, at].astype(jnp.float32) + skip[:, at] * grads).astype(
            jnp.bfloat16
        )

    def take(slot, landing, finish, tile):
        @pl.loop(0, half)
        def _(step):
            index = lax.rem(mine + step, half)
            at = cols(index, tile)
            other(
                near_first + index,
                lambda: wait_for(result_sem.at[slot, tile, index], landing.at[:, at]),
            )
            finish(at)

    def take_sums():
        @pl.loop(0, n)
        def _(device):
            for tile in range(2):
                other(
                    device,
                    lambda tile=tile: wait_for(sums_sem.at[device, tile], sums_in.at[device, tile]),
                )

        for index in range(half):
            for tile in range(2):
                sums_table[2 * index + tile] = sums_in[index, tile] + sums_in[half + index, tile]
        gain[...] = sums_table[owner[me]]

    for narrow in (True, False):

        @pl.loop(0, 2)
        def _(tile, narrow=narrow):
            @pl.when(lower if narrow else jnp.logical_not(lower))
            def _():
                take(0, conv_in, finish_conv, tile)

            @pl.when(jnp.logical_not(lower) if narrow else lower)
            def _():
                take(1, back_in, finish_back, tile)

            if narrow:
                for kind, count in (
                    (FILTER, n - 1),
                    (NARROW, half - 1),
                    (WIDE_NEAR, half - 1),
                    (WIDE_FAR, half),
                    (RESULT_NARROW, half - 1),
                ):
                    wait_for(send_sem.at[kind, tile], wide_in.at[tile, pl.ds(0, count)])
                wait_for(sums_send_sem.at[tile], sums_table.at[pl.ds(0, n - 1)])
            else:
                wait_for(send_sem.at[RESULT_WIDE, tile], wide_in.at[tile, pl.ds(0, half - 1)])

        if narrow:
            take_sums()


def finish_kernel(
    output_loc, value_grad_loc, gate_grad_loc, gain_loc, output, value_grad, gate_grad, gain, sem
):
    copies = [
        pltpu.make_async_copy(source, target, sem.at[index])
        for index, (source, target) in enumerate(
            (
                (output_loc, output),
                (value_grad_loc, value_grad),
                (gate_grad_loc, gate_grad),
                (gain_loc, gain),
            )
        )
    ]
    for copy in copies:
        copy.start()
    for copy in copies:
        copy.wait()


def fused_body(value, gate, long_filter, skip_gain, cotangent, owner_map):
    n = lax.axis_size("seq")
    rows, group = value.shape
    chans = group // n
    tables = block_tables(rows)
    anywhere = pl.BlockSpec(memory_space=pltpu.HBM)
    vmem = pl.BlockSpec(memory_space=pltpu.VMEM)
    bf16, f32 = jnp.bfloat16, jnp.float32
    half = n // 2
    half_spec = pltpu.VMEM((2, half, 2 * rows, chans), f32)
    tokens = pltpu.VMEM((rows, group), bf16)
    tiles = pltpu.VMEM((2, n, rows, chans), bf16)
    half_tiles = pltpu.VMEM((2, half, rows, chans), bf16)
    local = pl.pallas_call(
        functools.partial(fused_kernel, n),
        out_shape=(tokens, tokens, tokens, pltpu.VMEM((1, chans), f32)),
        in_specs=[anywhere] * 9,
        out_specs=(vmem,) * 4,
        scratch_shapes=[
            *(pltpu.VMEM(table.shape, bf16) for table in tables),
            pltpu.VMEM((1, group), f32),
            pltpu.SMEM(owner_map.shape, jnp.int32),
            tokens,
            tokens,
            tokens,
            tokens,
            pltpu.VMEM((2, n, chans, rows), bf16),
            half_tiles,
            tiles,
            pltpu.VMEM((n + 1, rows, chans), bf16),
            pltpu.VMEM((2, n, 2 * rows, chans), f32),
            pltpu.VMEM((half, 2 * rows, chans), f32),
            half_spec,
            half_spec,
            half_tiles,
            half_tiles,
            tokens,
            tokens,
            pltpu.VMEM((2, 1, chans), f32),
            pltpu.VMEM((n, 2, 1, chans), f32),
            pltpu.VMEM((n, 1, chans), f32),
            pltpu.SemaphoreType.DMA((KINDS, 2)),
            pltpu.SemaphoreType.DMA((KINDS, 2)),
            pltpu.SemaphoreType.DMA((2, 2, half)),
            pltpu.SemaphoreType.DMA((2,)),
            pltpu.SemaphoreType.DMA((n, 2)),
            pltpu.SemaphoreType.DMA((10,)),
        ],
        compiler_params=pltpu.CompilerParams(
            collective_id=0,
            has_side_effects=True,
            vmem_limit_bytes=DEVICE_VMEM - 6 * rows * group - 2**16,
        ),
    )(
        value,
        long_filter,
        gate,
        cotangent,
        skip_gain.reshape(1, group),
        owner_map,
        *tables,
    )
    result = jax.ShapeDtypeStruct((rows, group), bf16)
    output, value_grad, gate_grad, gain = pl.pallas_call(
        finish_kernel,
        out_shape=(result, result, result, jax.ShapeDtypeStruct((1, chans), f32)),
        in_specs=[vmem] * 4,
        out_specs=(anywhere,) * 4,
        scratch_shapes=[pltpu.SemaphoreType.DMA((4,))],
        compiler_params=pltpu.CompilerParams(vmem_limit_bytes=2**20),
    )(*local)
    return (output, value_grad, gate_grad, gain.reshape(1, 1, chans))


def body(value, gate, long_filter, skip_gain, cotangent, owner_map):
    n = lax.axis_size("seq")
    rows, group = value.shape
    aligned = rows % LANES == 0 and group % (n * LANES) == 0 and n % 4 == 0
    needed = 64 * rows * group + 48 * rows * rows
    chosen = fused_body if aligned and needed <= DEVICE_VMEM // 2 else split_body
    return chosen(value, gate, long_filter, skip_gain, cotangent, owner_map)


def solution(mesh):
    in_specs = (
        P("seq", "chan"),
        P("seq", "chan"),
        P("chan", "seq"),
        P("chan"),
        P("seq", "chan"),
        P(),
    )
    out_specs = (P("seq", "chan"), P("seq", "chan"), P("seq", "chan"), P("chan", "seq", None))
    return jax.shard_map(body, mesh=mesh, in_specs=in_specs, out_specs=out_specs, check_vma=False)
```

```python
import functools
import math

import jax
import jax.numpy as jnp
import numpy as np
from jax import lax
from jax.experimental import pallas as pl
from jax.experimental.pallas import tpu as pltpu
from jax.sharding import PartitionSpec as P

HIGHEST = lax.Precision.HIGHEST


def dft_table(size):
    index = jnp.arange(size, dtype=jnp.int32)
    phase = index[:, None] * index[None, :] % size
    angle = 2.0 * math.pi / size * phase.astype(jnp.float32)
    return (jnp.cos(angle), jnp.sin(angle))


def make_tables(outer, inner):
    cos_outer, sin_outer = dft_table(outer)
    cos_inner, sin_inner = dft_table(inner)
    total = outer * inner
    phase = (
        jnp.arange(outer, dtype=jnp.int32)[:, None]
        * jnp.arange(inner, dtype=jnp.int32)[None, :]
        % total
    )
    angle = 2.0 * math.pi / total * phase.astype(jnp.float32)
    return (cos_outer, sin_outer, cos_inner, sin_inner, jnp.cos(angle), jnp.sin(angle))


def forward_dft(signal, tables):
    cos_outer, sin_outer, cos_inner, sin_inner, turn_cos, turn_sin = tables
    blocks = signal.shape[0]
    real_part = jnp.einsum("kn,ncb->ckb", cos_outer[:, :blocks], signal, precision=HIGHEST)
    imag_part = -jnp.einsum("kn,ncb->ckb", sin_outer[:, :blocks], signal, precision=HIGHEST)
    twisted_real = real_part * turn_cos + imag_part * turn_sin
    twisted_imag = imag_part * turn_cos - real_part * turn_sin
    spec_real = jnp.einsum("ckn,nm->ckm", twisted_real, cos_inner, precision=HIGHEST) + jnp.einsum(
        "ckn,nm->ckm", twisted_imag, sin_inner, precision=HIGHEST
    )
    spec_imag = jnp.einsum("ckn,nm->ckm", twisted_imag, cos_inner, precision=HIGHEST) - jnp.einsum(
        "ckn,nm->ckm", twisted_real, sin_inner, precision=HIGHEST
    )
    return (spec_real, spec_imag)


def inverse_dft(spec_real, spec_imag, tables, blocks):
    cos_outer, sin_outer, cos_inner, sin_inner, turn_cos, turn_sin = tables
    total = cos_outer.shape[0] * cos_inner.shape[0]
    inner_real = jnp.einsum("ckm,mn->ckn", spec_real, cos_inner, precision=HIGHEST) - jnp.einsum(
        "ckm,mn->ckn", spec_imag, sin_inner, precision=HIGHEST
    )
    inner_imag = jnp.einsum("ckm,mn->ckn", spec_real, sin_inner, precision=HIGHEST) + jnp.einsum(
        "ckm,mn->ckn", spec_imag, cos_inner, precision=HIGHEST
    )
    turned_real = inner_real * turn_cos - inner_imag * turn_sin
    turned_imag = inner_real * turn_sin + inner_imag * turn_cos
    result = jnp.einsum(
        "nk,ckb->ncb", cos_outer[:blocks, :], turned_real, precision=HIGHEST
    ) - jnp.einsum("nk,ckb->ncb", sin_outer[:blocks, :], turned_imag, precision=HIGHEST)
    return result / total


def causal_conv(sent_value, filter_spec, tables):
    value_real, value_imag = forward_dft(sent_value.astype(jnp.float32), tables)
    filter_real, filter_imag = filter_spec
    product_real = value_real * filter_real - value_imag * filter_imag
    product_imag = value_real * filter_imag + value_imag * filter_real
    return inverse_dft(product_real, product_imag, tables, sent_value.shape[0]).astype(jnp.bfloat16)


def transposed_conv(sent_grad, filter_spec, tables):
    grad_real, grad_imag = forward_dft(sent_grad.astype(jnp.float32), tables)
    filter_real, filter_imag = filter_spec
    product_real = grad_real * filter_real + grad_imag * filter_imag
    product_imag = grad_imag * filter_real - grad_real * filter_imag
    return inverse_dft(product_real, product_imag, tables, sent_grad.shape[0]).astype(jnp.bfloat16)


def split_body(value, gate, long_filter, skip_gain, cotangent, owner_map):
    blocks = lax.axis_size("seq")
    tok_rows = value.shape[0]
    group = value.shape[1]
    per_device = group // blocks
    value_rows = value.astype(jnp.float32)
    gate_rows = gate.astype(jnp.float32)
    grad_rows = (cotangent.astype(jnp.float32) * gate_rows).astype(jnp.bfloat16)
    value_major = value.T
    grad_major = grad_rows.T
    tables = make_tables(2 * blocks, tok_rows)
    value_split = value_major.reshape(blocks, per_device, tok_rows)
    filter_split = long_filter.reshape(blocks, per_device, tok_rows)
    grad_split = grad_major.reshape(blocks, per_device, tok_rows)
    sent_value, sent_filter = (
        lax.all_to_all(value_split, "seq", split_axis=0, concat_axis=0, tiled=True),
        lax.all_to_all(filter_split, "seq", split_axis=0, concat_axis=0, tiled=True),
    )
    filter_spec = forward_dft(sent_filter.astype(jnp.float32), tables)
    conv_back = lax.all_to_all(
        causal_conv(sent_value, filter_spec, tables), "seq", split_axis=0, concat_axis=0, tiled=True
    )
    sent_grad = lax.all_to_all(grad_split, "seq", split_axis=0, concat_axis=0, tiled=True)
    grad_back = lax.all_to_all(
        transposed_conv(sent_grad, filter_spec, tables),
        "seq",
        split_axis=0,
        concat_axis=0,
        tiled=True,
    )
    conv_rows = conv_back.reshape(group, tok_rows).T.astype(jnp.float32)
    mixed = conv_rows + skip_gain * value_rows
    output = (gate_rows * mixed).astype(jnp.bfloat16)
    gate_grad = (cotangent.astype(jnp.float32) * mixed).astype(jnp.bfloat16)
    back_rows = grad_back.reshape(group, tok_rows).T.astype(jnp.float32)
    grad_float = grad_rows.astype(jnp.float32)
    value_grad = (back_rows + skip_gain * grad_float).astype(jnp.bfloat16)
    scale = 1.0 / math.sqrt(tok_rows * blocks)
    local_sums = (
        jnp.sum(sent_value.astype(jnp.float32) * sent_grad.astype(jnp.float32), axis=(0, 2)) * scale
    )
    gathered = lax.all_gather(local_sums.reshape(1, per_device), "seq", axis=0, tiled=True)
    mine = owner_map[lax.axis_index("seq")]
    summed = lax.dynamic_slice_in_dim(gathered, mine, 1, 0)
    gain_grad = summed.reshape(1, 1, per_device)
    return (output, value_grad, gate_grad, gain_grad)


LANES = 128
DEVICE_VMEM = 67043328
FILTER, NARROW, WIDE_NEAR, WIDE_FAR, RESULT_NARROW, RESULT_WIDE, KINDS = range(7)
MESH = pl.DeviceIdType.MESH


def block_tables(rows):
    angle = math.pi / (2 * rows) * (2 * np.arange(rows, dtype=np.float64)[:, None] + 1)
    tokens = angle * np.arange(rows, dtype=np.float64)[None, :]
    window = angle * np.arange(-rows, rows, dtype=np.float64)[None, :]

    def parts(wide):
        high = wide.astype(jnp.bfloat16)
        return high, (wide - high.astype(np.float64)).astype(jnp.bfloat16)

    signal_high, signal_low = parts(np.concatenate([np.cos(tokens), -np.sin(tokens)]))
    window_high, window_low = parts(np.concatenate([np.cos(window), -np.sin(window)]))
    back = np.concatenate([np.cos(tokens), -np.sin(tokens)]).T / rows
    back_high, back_low = parts(back)
    return (
        np.concatenate([signal_high, signal_low], axis=1),
        np.concatenate([window_high, window_low], axis=1),
        np.concatenate([back_high, back_low, back_high], axis=1),
    )


def fused_kernel(
    n,
    value,
    filt,
    gate,
    cot,
    skip_any,
    owner_any,
    signal_any,
    window_any,
    back_any,
    output,
    value_grad,
    gate_grad,
    gain,
    signal_table,
    window_table,
    back_table,
    skip,
    owner,
    value_loc,
    gate_loc,
    cot_loc,
    grad_loc,
    filter_in,
    narrow_in,
    wide_in,
    taps,
    spec_filter,
    spec_signal,
    product_narrow,
    product_wide,
    narrow_out,
    wide_out,
    conv_in,
    back_in,
    sums_out,
    sums_in,
    sums_table,
    send_sem,
    recv_sem,
    result_sem,
    sums_send_sem,
    sums_sem,
    local_sem,
):
    me = lax.axis_index("seq")
    half = n // 2
    rows, group = value.shape
    chans = group // n
    length = rows * n
    lower = me < half
    mirror = n - 1 - me
    mine = lax.rem(me, half)
    place = jnp.where(lower, me, mirror)
    near_first = jnp.where(lower, 0, half)

    def cols(index, tile):
        return pl.ds(pl.multiple_of((2 * index + tile) * chans, chans), chans)

    def other(device, action):
        @pl.when(device != me)
        def _():
            action()

    def start(source, target, device, sent, arrival):
        def action():
            pltpu.make_async_remote_copy(
                src_ref=source,
                dst_ref=target,
                send_sem=sent,
                recv_sem=arrival,
                device_id={"seq": device},
                device_id_type=MESH,
            ).start()

        other(device, action)

    def wait_for(semaphore, blocks):
        pltpu.make_async_copy(blocks, blocks, semaphore).wait()

    barrier = pltpu.get_barrier_semaphore()

    @pl.loop(0, n)
    def _(device):
        def greet():
            pl.semaphore_signal(barrier, inc=1, device_id={"seq": device}, device_id_type=MESH)

        other(device, greet)

    local = [
        pltpu.make_async_copy(gate, gate_loc, local_sem.at[0]),
        pltpu.make_async_copy(cot, cot_loc, local_sem.at[1]),
        pltpu.make_async_copy(value, value_loc, local_sem.at[2]),
        pltpu.make_async_copy(signal_any, signal_table, local_sem.at[3]),
        pltpu.make_async_copy(window_any, window_table, local_sem.at[4]),
        pltpu.make_async_copy(back_any, back_table, local_sem.at[5]),
        pltpu.make_async_copy(skip_any, skip, local_sem.at[6]),
        pltpu.make_async_copy(owner_any, owner, local_sem.at[7]),
        pltpu.make_async_copy(filt.at[cols(mine, 0), :], filter_in.at[0, me], local_sem.at[8]),
        pltpu.make_async_copy(filt.at[cols(mine, 1), :], filter_in.at[1, me], local_sem.at[9]),
    ]
    for copy in local:
        copy.start()
    pl.semaphore_wait(barrier, n - 1)

    def turn(step):
        away = jnp.where(step < half // 2, half - 1 - 2 * step, 2 * (half - 1 - step))
        return lax.rem(mine // 2 + away // 2, half // 2) * 2 + lax.rem(mine + away, 2)

    def send(kind, source_of, target, tile, far):
        first = half - near_first if far else near_first

        @pl.loop(0, half)
        def _(step):
            index = turn(step)
            start(
                source_of(index),
                target,
                first + index,
                send_sem.at[kind, tile],
                recv_sem.at[kind, tile],
            )

    def send_filter(tile, far):
        send(FILTER, lambda i: filt.at[cols(i, tile), :], filter_in.at[tile, me], tile, far)

    def send_value(tile, far, near):
        def source(index):
            return value.at[:, cols(index, tile)]

        @pl.when(lower)
        def _():
            if far:
                send(WIDE_FAR, source, wide_in.at[tile, me], tile, True)
            if near:
                send(NARROW, source, narrow_in.at[tile, me], tile, False)

        if near:

            @pl.when(jnp.logical_not(lower))
            def _():
                send(WIDE_NEAR, source, wide_in.at[tile, me], tile, False)

    def send_grad(tile, far, near):
        def source(index):
            return grad_loc.at[:, cols(index, tile)]

        @pl.when(jnp.logical_not(lower))
        def _():
            if far:
                send(WIDE_FAR, source, wide_in.at[tile, mirror], tile, True)
            if near:
                send(NARROW, source, narrow_in.at[tile, mirror], tile, False)

        if near:

            @pl.when(lower)
            def _():
                send(WIDE_NEAR, source, wide_in.at[tile, mirror], tile, False)

    def make_grads():
        local[0].wait()
        local[1].wait()

        @pl.loop(0, rows // 16)
        def _(step):
            at = pl.ds(pl.multiple_of(step * 16, 16), 16)
            grads = cot_loc[at, :].astype(jnp.float32) * gate_loc[at, :].astype(jnp.float32)
            grad_loc[at, :] = grads.astype(jnp.bfloat16)

    @pl.loop(0, 2)
    def _(tile):
        send_filter(tile, True)
        send_filter(tile, False)

    make_grads()

    @pl.loop(0, 2)
    def _(tile):
        send_value(tile, False, True)
        send_grad(tile, False, True)

    @pl.loop(0, 2)
    def _(tile):
        send_value(tile, True, False)
        send_grad(tile, True, False)
    for copy in local[2:]:
        copy.wait()

    def dot(left, right):
        return jnp.dot(left, right, preferred_element_type=jnp.float32)

    def spectrum(signal, tile, first):
        @pl.loop(0, half, step=2, unroll=True)
        def _(block):
            pair = jnp.concatenate(
                [signal[tile, first + block], signal[tile, first + block + 1]], axis=1
            )
            both = dot(signal_table[...], jnp.concatenate([pair, pair], axis=0))
            spec_signal[block] = both[:, :chans]
            spec_signal[block + 1] = both[:, chans:]

    def multiply(result, tile, sign, pairs, windows, adds):
        @pl.loop(0, rows // 8)
        def _(step):
            real = pl.ds(pl.multiple_of(step * 8, 8), 8)
            imag = pl.ds(pl.multiple_of(rows + step * 8, 8), 8)
            signal_real = [spec_signal[c, real, :] for c in range(half)]
            signal_imag = [spec_signal[c, imag, :] for c in range(half)]
            filter_real = {d: spec_filter[tile, d, real, :] for d in windows}
            filter_imag = {d: spec_filter[tile, d, imag, :] * sign for d in windows}
            for block in range(half):
                total_real = result[tile, block, real, :] if adds else None
                total_imag = result[tile, block, imag, :] if adds else None
                for c, d in pairs(block):
                    with_real, with_imag = filter_real[d], filter_imag[d]
                    term_real = signal_real[c] * with_real - signal_imag[c] * with_imag
                    term_imag = signal_imag[c] * with_real + signal_real[c] * with_imag
                    total_real = term_real if total_real is None else total_real + term_real
                    total_imag = term_imag if total_imag is None else total_imag + term_imag
                result[tile, block, real, :] = total_real
                result[tile, block, imag, :] = total_imag

    def multiply_near(result, tile, sign):
        multiply(
            result, tile, sign, lambda b: [(c, b - c) for c in range(b + 1)], range(half), False
        )

    def multiply_far(result, tile, sign):
        multiply(
            result,
            tile,
            sign,
            lambda b: [(c, half + b - c) for c in range(half)],
            range(1, n),
            True,
        )

    def inverse(product, result, tile):
        @pl.loop(0, half, step=2, unroll=True)
        def _(block):
            wide = jnp.concatenate([product[tile, block], product[tile, block + 1]], axis=1)
            high = wide.astype(jnp.bfloat16)
            low = (wide - high.astype(jnp.float32)).astype(jnp.bfloat16)
            both = dot(back_table[...], jnp.concatenate([high, high, low], axis=0))
            result[tile, block] = both[:, :chans].astype(jnp.bfloat16)
            result[tile, block + 1] = both[:, chans:].astype(jnp.bfloat16)

    def filter_spectra(tile):
        wait_for(recv_sem.at[FILTER, tile], filter_in.at[tile, pl.ds(0, n - 1)])
        taps[0] = jnp.zeros(taps.shape[1:], jnp.bfloat16)

        @pl.loop(0, n, unroll=True)
        def _(block):
            taps[block + 1] = filter_in[tile, block].astype(jnp.float32).T.astype(jnp.bfloat16)

        @pl.loop(0, n, step=2, unroll=True)
        def _(block):
            before, here, after = taps[block], taps[block + 1], taps[block + 2]
            pair = jnp.concatenate(
                [
                    jnp.concatenate([before, here], axis=0),
                    jnp.concatenate([here, after], axis=0),
                ],
                axis=1,
            )
            both = dot(window_table[...], jnp.concatenate([pair, pair], axis=0))
            spec_filter[tile, block] = both[:, :chans]
            spec_filter[tile, block + 1] = both[:, chans:]

    def send_results(kind, source_of, target, slot, tile):
        @pl.loop(0, half)
        def _(step):
            index = turn(step)
            start(
                source_of(index),
                target.at[:, cols(mine, tile)],
                near_first + index,
                send_sem.at[kind, tile],
                result_sem.at[slot, tile, mine],
            )

        target[:, cols(mine, tile)] = source_of(mine)[...]

    def narrow_results(tile):
        @pl.when(lower)
        def _():
            narrow_in[tile, place] = value_loc[:, cols(mine, tile)]

        @pl.when(jnp.logical_not(lower))
        def _():
            narrow_in[tile, place] = grad_loc[:, cols(mine, tile)]

        wait_for(recv_sem.at[NARROW, tile], narrow_in.at[tile, pl.ds(0, half - 1)])
        spectrum(narrow_in, tile, 0)
        multiply_near(product_narrow, tile, jnp.where(lower, 1.0, -1.0))
        inverse(product_narrow, narrow_out, tile)

        @pl.when(lower)
        def _():
            send_results(RESULT_NARROW, lambda index: narrow_out.at[tile, index], conv_in, 0, tile)

        @pl.when(jnp.logical_not(lower))
        def _():
            send_results(RESULT_NARROW, lambda index: narrow_out.at[tile, half - 1 - index], back_in, 1, tile)

    def wide_near(tile):
        @pl.when(lower)
        def _():
            wide_in[tile, mirror] = grad_loc[:, cols(mine, tile)]

        @pl.when(jnp.logical_not(lower))
        def _():
            wide_in[tile, me] = value_loc[:, cols(mine, tile)]

        wait_for(recv_sem.at[WIDE_NEAR, tile], wide_in.at[tile, pl.ds(0, half - 1)])
        tile_sums(tile)
        spectrum(wide_in, tile, half)
        multiply_near(product_wide, tile, jnp.where(lower, -1.0, 1.0))

    def wide_results(tile):
        wait_for(recv_sem.at[WIDE_FAR, tile], wide_in.at[tile, pl.ds(0, half)])
        spectrum(wide_in, tile, 0)
        multiply_far(product_wide, tile, jnp.where(lower, -1.0, 1.0))
        inverse(product_wide, wide_out, tile)

        @pl.when(lower)
        def _():
            send_results(RESULT_WIDE, lambda index: wide_out.at[tile, half - 1 - index], back_in, 1, tile)

        @pl.when(jnp.logical_not(lower))
        def _():
            send_results(RESULT_WIDE, lambda index: wide_out.at[tile, index], conv_in, 0, tile)

    def tile_sums(tile):
        @pl.loop(0, rows // 16, init_carry=jnp.zeros((16, chans), jnp.float32))
        def total(step, carry):
            at = pl.ds(pl.multiple_of(step * 16, 16), 16)
            for block in range(half):
                carry += narrow_in[tile, block, at, :].astype(jnp.float32) * wide_in[
                    tile, n - 1 - block, at, :
                ].astype(jnp.float32)
            return carry

        sums_out[tile] = jnp.sum(total, axis=0, keepdims=True) * (1.0 / math.sqrt(length))
        sums_in[me, tile] = sums_out[tile]

        @pl.loop(0, n)
        def _(device):
            start(
                sums_out.at[tile],
                sums_in.at[me, tile],
                device,
                sums_send_sem.at[tile],
                sums_sem.at[me, tile],
            )

    for stage in (filter_spectra, narrow_results, wide_near, wide_results):
        pl.loop(0, 2)(stage)

    def finish_conv(at):
        cot_rows = cot_loc[:, at].astype(jnp.float32)
        gate_rows = gate_loc[:, at].astype(jnp.float32)
        mixed = conv_in[:, at].astype(jnp.float32) + skip[:, at] * value_loc[:, at].astype(
            jnp.float32
        )
        output[:, at] = (gate_rows * mixed).astype(jnp.bfloat16)
        gate_grad[:, at] = (cot_rows * mixed).astype(jnp.bfloat16)

    def finish_back(at):
        grads = grad_loc[:, at].astype(jnp.float32)
        value_grad[:, at] = (back_in[:, at].astype(jnp.float32) + skip[:, at] * grads).astype(
            jnp.bfloat16
        )

    def take(slot, landing, finish, tile):
        @pl.loop(0, half)
        def _(step):
            index = lax.rem(mine + step, half)
            at = cols(index, tile)
            other(
                near_first + index,
                lambda: wait_for(result_sem.at[slot, tile, index], landing.at[:, at]),
            )
            finish(at)

    def take_sums():
        @pl.loop(0, n)
        def _(device):
            for tile in range(2):
                other(
                    device,
                    lambda tile=tile: wait_for(sums_sem.at[device, tile], sums_in.at[device, tile]),
                )

        for index in range(half):
            for tile in range(2):
                sums_table[2 * index + tile] = sums_in[index, tile] + sums_in[half + index, tile]
        gain[...] = sums_table[owner[me]]

    for narrow in (True, False):

        @pl.loop(0, 2)
        def _(tile, narrow=narrow):
            @pl.when(lower if narrow else jnp.logical_not(lower))
            def _():
                take(0, conv_in, finish_conv, tile)

            @pl.when(jnp.logical_not(lower) if narrow else lower)
            def _():
                take(1, back_in, finish_back, tile)

            if narrow:
                for kind, count in (
                    (FILTER, n - 1),
                    (NARROW, half - 1),
                    (WIDE_NEAR, half - 1),
                    (WIDE_FAR, half),
                    (RESULT_NARROW, half - 1),
                ):
                    wait_for(send_sem.at[kind, tile], wide_in.at[tile, pl.ds(0, count)])
                wait_for(sums_send_sem.at[tile], sums_table.at[pl.ds(0, n - 1)])
            else:
                wait_for(send_sem.at[RESULT_WIDE, tile], wide_in.at[tile, pl.ds(0, half - 1)])

        if narrow:
            take_sums()


def finish_kernel(
    output_loc, value_grad_loc, gate_grad_loc, gain_loc, output, value_grad, gate_grad, gain, sem
):
    copies = [
        pltpu.make_async_copy(source, target, sem.at[index])
        for index, (source, target) in enumerate(
            (
                (output_loc, output),
                (value_grad_loc, value_grad),
                (gate_grad_loc, gate_grad),
                (gain_loc, gain),
            )
        )
    ]
    for copy in copies:
        copy.start()
    for copy in copies:
        copy.wait()


def fused_body(value, gate, long_filter, skip_gain, cotangent, owner_map):
    n = lax.axis_size("seq")
    rows, group = value.shape
    chans = group // n
    tables = block_tables(rows)
    anywhere = pl.BlockSpec(memory_space=pltpu.HBM)
    vmem = pl.BlockSpec(memory_space=pltpu.VMEM)
    bf16, f32 = jnp.bfloat16, jnp.float32
    half = n // 2
    half_spec = pltpu.VMEM((2, half, 2 * rows, chans), f32)
    tokens = pltpu.VMEM((rows, group), bf16)
    tiles = pltpu.VMEM((2, n, rows, chans), bf16)
    half_tiles = pltpu.VMEM((2, half, rows, chans), bf16)
    local = pl.pallas_call(
        functools.partial(fused_kernel, n),
        out_shape=(tokens, tokens, tokens, pltpu.VMEM((1, chans), f32)),
        in_specs=[anywhere] * 9,
        out_specs=(vmem,) * 4,
        scratch_shapes=[
            *(pltpu.VMEM(table.shape, bf16) for table in tables),
            pltpu.VMEM((1, group), f32),
            pltpu.SMEM(owner_map.shape, jnp.int32),
            tokens,
            tokens,
            tokens,
            tokens,
            pltpu.VMEM((2, n, chans, rows), bf16),
            half_tiles,
            tiles,
            pltpu.VMEM((n + 1, rows, chans), bf16),
            pltpu.VMEM((2, n, 2 * rows, chans), f32),
            pltpu.VMEM((half, 2 * rows, chans), f32),
            half_spec,
            half_spec,
            half_tiles,
            half_tiles,
            tokens,
            tokens,
            pltpu.VMEM((2, 1, chans), f32),
            pltpu.VMEM((n, 2, 1, chans), f32),
            pltpu.VMEM((n, 1, chans), f32),
            pltpu.SemaphoreType.DMA((KINDS, 2)),
            pltpu.SemaphoreType.DMA((KINDS, 2)),
            pltpu.SemaphoreType.DMA((2, 2, half)),
            pltpu.SemaphoreType.DMA((2,)),
            pltpu.SemaphoreType.DMA((n, 2)),
            pltpu.SemaphoreType.DMA((10,)),
        ],
        compiler_params=pltpu.CompilerParams(
            collective_id=0,
            has_side_effects=True,
            vmem_limit_bytes=DEVICE_VMEM - 6 * rows * group - 2**16,
        ),
    )(
        value,
        long_filter,
        gate,
        cotangent,
        skip_gain.reshape(1, group),
        owner_map,
        *tables,
    )
    result = jax.ShapeDtypeStruct((rows, group), bf16)
    output, value_grad, gate_grad, gain = pl.pallas_call(
        finish_kernel,
        out_shape=(result, result, result, jax.ShapeDtypeStruct((1, chans), f32)),
        in_specs=[vmem] * 4,
        out_specs=(anywhere,) * 4,
        scratch_shapes=[pltpu.SemaphoreType.DMA((4,))],
        compiler_params=pltpu.CompilerParams(vmem_limit_bytes=2**20),
    )(*local)
    return (output, value_grad, gate_grad, gain.reshape(1, 1, chans))


def body(value, gate, long_filter, skip_gain, cotangent, owner_map):
    n = lax.axis_size("seq")
    rows, group = value.shape
    aligned = rows % LANES == 0 and group % (n * LANES) == 0 and n % 4 == 0
    needed = 64 * rows * group + 48 * rows * rows
    chosen = fused_body if aligned and needed <= DEVICE_VMEM // 2 else split_body
    return chosen(value, gate, long_filter, skip_gain, cotangent, owner_map)


def solution(mesh):
    in_specs = (
        P("seq", "chan"),
        P("seq", "chan"),
        P("chan", "seq"),
        P("chan"),
        P("seq", "chan"),
        P(),
    )
    out_specs = (P("seq", "chan"), P("seq", "chan"), P("seq", "chan"), P("chan", "seq", None))
    return jax.shard_map(body, mesh=mesh, in_specs=in_specs, out_specs=out_specs, check_vma=False)
```

```python
import functools
import math

import jax
import jax.numpy as jnp
import numpy as np
from jax import lax
from jax.experimental import pallas as pl
from jax.experimental.pallas import tpu as pltpu
from jax.sharding import PartitionSpec as P

HIGHEST = lax.Precision.HIGHEST


def dft_table(size):
    index = jnp.arange(size, dtype=jnp.int32)
    phase = index[:, None] * index[None, :] % size
    angle = 2.0 * math.pi / size * phase.astype(jnp.float32)
    return (jnp.cos(angle), jnp.sin(angle))


def make_tables(outer, inner):
    cos_outer, sin_outer = dft_table(outer)
    cos_inner, sin_inner = dft_table(inner)
    total = outer * inner
    phase = (
        jnp.arange(outer, dtype=jnp.int32)[:, None]
        * jnp.arange(inner, dtype=jnp.int32)[None, :]
        % total
    )
    angle = 2.0 * math.pi / total * phase.astype(jnp.float32)
    return (cos_outer, sin_outer, cos_inner, sin_inner, jnp.cos(angle), jnp.sin(angle))


def forward_dft(signal, tables):
    cos_outer, sin_outer, cos_inner, sin_inner, turn_cos, turn_sin = tables
    blocks = signal.shape[0]
    real_part = jnp.einsum("kn,ncb->ckb", cos_outer[:, :blocks], signal, precision=HIGHEST)
    imag_part = -jnp.einsum("kn,ncb->ckb", sin_outer[:, :blocks], signal, precision=HIGHEST)
    twisted_real = real_part * turn_cos + imag_part * turn_sin
    twisted_imag = imag_part * turn_cos - real_part * turn_sin
    spec_real = jnp.einsum("ckn,nm->ckm", twisted_real, cos_inner, precision=HIGHEST) + jnp.einsum(
        "ckn,nm->ckm", twisted_imag, sin_inner, precision=HIGHEST
    )
    spec_imag = jnp.einsum("ckn,nm->ckm", twisted_imag, cos_inner, precision=HIGHEST) - jnp.einsum(
        "ckn,nm->ckm", twisted_real, sin_inner, precision=HIGHEST
    )
    return (spec_real, spec_imag)


def inverse_dft(spec_real, spec_imag, tables, blocks):
    cos_outer, sin_outer, cos_inner, sin_inner, turn_cos, turn_sin = tables
    total = cos_outer.shape[0] * cos_inner.shape[0]
    inner_real = jnp.einsum("ckm,mn->ckn", spec_real, cos_inner, precision=HIGHEST) - jnp.einsum(
        "ckm,mn->ckn", spec_imag, sin_inner, precision=HIGHEST
    )
    inner_imag = jnp.einsum("ckm,mn->ckn", spec_real, sin_inner, precision=HIGHEST) + jnp.einsum(
        "ckm,mn->ckn", spec_imag, cos_inner, precision=HIGHEST
    )
    turned_real = inner_real * turn_cos - inner_imag * turn_sin
    turned_imag = inner_real * turn_sin + inner_imag * turn_cos
    result = jnp.einsum(
        "nk,ckb->ncb", cos_outer[:blocks, :], turned_real, precision=HIGHEST
    ) - jnp.einsum("nk,ckb->ncb", sin_outer[:blocks, :], turned_imag, precision=HIGHEST)
    return result / total


def causal_conv(sent_value, filter_spec, tables):
    value_real, value_imag = forward_dft(sent_value.astype(jnp.float32), tables)
    filter_real, filter_imag = filter_spec
    product_real = value_real * filter_real - value_imag * filter_imag
    product_imag = value_real * filter_imag + value_imag * filter_real
    return inverse_dft(product_real, product_imag, tables, sent_value.shape[0]).astype(jnp.bfloat16)


def transposed_conv(sent_grad, filter_spec, tables):
    grad_real, grad_imag = forward_dft(sent_grad.astype(jnp.float32), tables)
    filter_real, filter_imag = filter_spec
    product_real = grad_real * filter_real + grad_imag * filter_imag
    product_imag = grad_imag * filter_real - grad_real * filter_imag
    return inverse_dft(product_real, product_imag, tables, sent_grad.shape[0]).astype(jnp.bfloat16)


def split_body(value, gate, long_filter, skip_gain, cotangent, owner_map):
    blocks = lax.axis_size("seq")
    tok_rows = value.shape[0]
    group = value.shape[1]
    per_device = group // blocks
    value_rows = value.astype(jnp.float32)
    gate_rows = gate.astype(jnp.float32)
    grad_rows = (cotangent.astype(jnp.float32) * gate_rows).astype(jnp.bfloat16)
    value_major = value.T
    grad_major = grad_rows.T
    tables = make_tables(2 * blocks, tok_rows)
    value_split = value_major.reshape(blocks, per_device, tok_rows)
    filter_split = long_filter.reshape(blocks, per_device, tok_rows)
    grad_split = grad_major.reshape(blocks, per_device, tok_rows)
    sent_value, sent_filter = (
        lax.all_to_all(value_split, "seq", split_axis=0, concat_axis=0, tiled=True),
        lax.all_to_all(filter_split, "seq", split_axis=0, concat_axis=0, tiled=True),
    )
    filter_spec = forward_dft(sent_filter.astype(jnp.float32), tables)
    conv_back = lax.all_to_all(
        causal_conv(sent_value, filter_spec, tables), "seq", split_axis=0, concat_axis=0, tiled=True
    )
    sent_grad = lax.all_to_all(grad_split, "seq", split_axis=0, concat_axis=0, tiled=True)
    grad_back = lax.all_to_all(
        transposed_conv(sent_grad, filter_spec, tables),
        "seq",
        split_axis=0,
        concat_axis=0,
        tiled=True,
    )
    conv_rows = conv_back.reshape(group, tok_rows).T.astype(jnp.float32)
    mixed = conv_rows + skip_gain * value_rows
    output = (gate_rows * mixed).astype(jnp.bfloat16)
    gate_grad = (cotangent.astype(jnp.float32) * mixed).astype(jnp.bfloat16)
    back_rows = grad_back.reshape(group, tok_rows).T.astype(jnp.float32)
    grad_float = grad_rows.astype(jnp.float32)
    value_grad = (back_rows + skip_gain * grad_float).astype(jnp.bfloat16)
    scale = 1.0 / math.sqrt(tok_rows * blocks)
    local_sums = (
        jnp.sum(sent_value.astype(jnp.float32) * sent_grad.astype(jnp.float32), axis=(0, 2)) * scale
    )
    gathered = lax.all_gather(local_sums.reshape(1, per_device), "seq", axis=0, tiled=True)
    mine = owner_map[lax.axis_index("seq")]
    summed = lax.dynamic_slice_in_dim(gathered, mine, 1, 0)
    gain_grad = summed.reshape(1, 1, per_device)
    return (output, value_grad, gate_grad, gain_grad)


LANES = 128
DEVICE_VMEM = 67043328
FILTER, NARROW, WIDE_NEAR, WIDE_FAR, RESULT_NARROW, RESULT_WIDE, KINDS = range(7)
MESH = pl.DeviceIdType.MESH


def block_tables(rows):
    angle = math.pi / (2 * rows) * (2 * np.arange(rows, dtype=np.float64)[:, None] + 1)
    tokens = angle * np.arange(rows, dtype=np.float64)[None, :]
    window = angle * np.arange(-rows, rows, dtype=np.float64)[None, :]

    def parts(wide):
        high = wide.astype(jnp.bfloat16)
        return high, (wide - high.astype(np.float64)).astype(jnp.bfloat16)

    signal_high, signal_low = parts(np.concatenate([np.cos(tokens), -np.sin(tokens)]))
    window_high, window_low = parts(np.concatenate([np.cos(window), -np.sin(window)]))
    back = np.concatenate([np.cos(tokens), -np.sin(tokens)]).T / rows
    back_high, back_low = parts(back)
    return (
        np.concatenate([signal_high, signal_low], axis=1),
        np.concatenate([window_high, window_low], axis=1),
        np.concatenate([back_high, back_low, back_high], axis=1),
    )


def fused_kernel(
    n,
    value,
    filt,
    gate,
    cot,
    skip_any,
    owner_any,
    signal_any,
    window_any,
    back_any,
    output,
    value_grad,
    gate_grad,
    gain,
    signal_table,
    window_table,
    back_table,
    skip,
    owner,
    value_loc,
    gate_loc,
    cot_loc,
    grad_loc,
    filter_in,
    narrow_in,
    wide_in,
    taps,
    spec_filter,
    spec_signal,
    product_narrow,
    product_wide,
    narrow_out,
    wide_out,
    conv_in,
    back_in,
    sums_out,
    sums_in,
    sums_table,
    send_sem,
    recv_sem,
    result_sem,
    sums_send_sem,
    sums_sem,
    local_sem,
):
    me = lax.axis_index("seq")
    half = n // 2
    rows, group = value.shape
    chans = group // n
    length = rows * n
    lower = me < half
    mirror = n - 1 - me
    mine = lax.rem(me, half)
    place = jnp.where(lower, me, mirror)
    near_first = jnp.where(lower, 0, half)

    def cols(index, tile):
        return pl.ds(pl.multiple_of((2 * index + tile) * chans, chans), chans)

    def other(device, action):
        @pl.when(device != me)
        def _():
            action()

    def start(source, target, device, sent, arrival):
        def action():
            pltpu.make_async_remote_copy(
                src_ref=source,
                dst_ref=target,
                send_sem=sent,
                recv_sem=arrival,
                device_id={"seq": device},
                device_id_type=MESH,
            ).start()

        other(device, action)

    def wait_for(semaphore, blocks):
        pltpu.make_async_copy(blocks, blocks, semaphore).wait()

    barrier = pltpu.get_barrier_semaphore()

    @pl.loop(0, n)
    def _(device):
        def greet():
            pl.semaphore_signal(barrier, inc=1, device_id={"seq": device}, device_id_type=MESH)

        other(device, greet)

    local = [
        pltpu.make_async_copy(gate, gate_loc, local_sem.at[0]),
        pltpu.make_async_copy(cot, cot_loc, local_sem.at[1]),
        pltpu.make_async_copy(value, value_loc, local_sem.at[2]),
        pltpu.make_async_copy(signal_any, signal_table, local_sem.at[3]),
        pltpu.make_async_copy(window_any, window_table, local_sem.at[4]),
        pltpu.make_async_copy(back_any, back_table, local_sem.at[5]),
        pltpu.make_async_copy(skip_any, skip, local_sem.at[6]),
        pltpu.make_async_copy(owner_any, owner, local_sem.at[7]),
        pltpu.make_async_copy(filt.at[cols(mine, 0), :], filter_in.at[0, me], local_sem.at[8]),
        pltpu.make_async_copy(filt.at[cols(mine, 1), :], filter_in.at[1, me], local_sem.at[9]),
    ]
    for copy in local:
        copy.start()
    pl.semaphore_wait(barrier, n - 1)

    def turn(step):
        away = jnp.where(step < half // 2, half - 1 - 2 * step, 2 * (half - 1 - step))
        return lax.rem(mine // 2 + away // 2, half // 2) * 2 + lax.rem(mine + away, 2)

    def send(kind, source_of, target, tile, far):
        first = half - near_first if far else near_first

        @pl.loop(0, half)
        def _(step):
            index = turn(step)
            start(
                source_of(index),
                target,
                first + index,
                send_sem.at[kind, tile],
                recv_sem.at[kind, tile],
            )

    def send_filter(tile, far):
        send(FILTER, lambda i: filt.at[cols(i, tile), :], filter_in.at[tile, me], tile, far)

    def send_value(tile, far, near):
        def source(index):
            return value.at[:, cols(index, tile)]

        @pl.when(lower)
        def _():
            if far:
                send(WIDE_FAR, source, wide_in.at[tile, me], tile, True)
            if near:
                send(NARROW, source, narrow_in.at[tile, me], tile, False)

        if near:

            @pl.when(jnp.logical_not(lower))
            def _():
                send(WIDE_NEAR, source, wide_in.at[tile, me], tile, False)

    def send_grad(tile, far, near):
        def source(index):
            return grad_loc.at[:, cols(index, tile)]

        @pl.when(jnp.logical_not(lower))
        def _():
            if far:
                send(WIDE_FAR, source, wide_in.at[tile, mirror], tile, True)
            if near:
                send(NARROW, source, narrow_in.at[tile, mirror], tile, False)

        if near:

            @pl.when(lower)
            def _():
                send(WIDE_NEAR, source, wide_in.at[tile, mirror], tile, False)

    def make_grads():
        local[0].wait()
        local[1].wait()

        @pl.loop(0, rows // 16)
        def _(step):
            at = pl.ds(pl.multiple_of(step * 16, 16), 16)
            grads = cot_loc[at, :].astype(jnp.float32) * gate_loc[at, :].astype(jnp.float32)
            grad_loc[at, :] = grads.astype(jnp.bfloat16)

    @pl.loop(0, 2)
    def _(tile):
        send_filter(tile, True)
        send_filter(tile, False)

    make_grads()

    @pl.loop(0, 2)
    def _(tile):
        send_value(tile, False, True)
        send_grad(tile, False, True)
        send_value(tile, True, False)
        send_grad(tile, True, False)
    for copy in local[2:]:
        copy.wait()

    def dot(left, right):
        return jnp.dot(left, right, preferred_element_type=jnp.float32)

    def spectrum(signal, tile, first):
        @pl.loop(0, half, step=2, unroll=True)
        def _(block):
            pair = jnp.concatenate(
                [signal[tile, first + block], signal[tile, first + block + 1]], axis=1
            )
            both = dot(signal_table[...], jnp.concatenate([pair, pair], axis=0))
            spec_signal[block] = both[:, :chans]
            spec_signal[block + 1] = both[:, chans:]

    def multiply(result, tile, sign, pairs, windows, adds):
        @pl.loop(0, rows // 8)
        def _(step):
            real = pl.ds(pl.multiple_of(step * 8, 8), 8)
            imag = pl.ds(pl.multiple_of(rows + step * 8, 8), 8)
            signal_real = [spec_signal[c, real, :] for c in range(half)]
            signal_imag = [spec_signal[c, imag, :] for c in range(half)]
            filter_real = {d: spec_filter[tile, d, real, :] for d in windows}
            filter_imag = {d: spec_filter[tile, d, imag, :] * sign for d in windows}
            for block in range(half):
                total_real = result[tile, block, real, :] if adds else None
                total_imag = result[tile, block, imag, :] if adds else None
                for c, d in pairs(block):
                    with_real, with_imag = filter_real[d], filter_imag[d]
                    term_real = signal_real[c] * with_real - signal_imag[c] * with_imag
                    term_imag = signal_imag[c] * with_real + signal_real[c] * with_imag
                    total_real = term_real if total_real is None else total_real + term_real
                    total_imag = term_imag if total_imag is None else total_imag + term_imag
                result[tile, block, real, :] = total_real
                result[tile, block, imag, :] = total_imag

    def multiply_near(result, tile, sign):
        multiply(
            result, tile, sign, lambda b: [(c, b - c) for c in range(b + 1)], range(half), False
        )

    def multiply_far(result, tile, sign):
        multiply(
            result,
            tile,
            sign,
            lambda b: [(c, half + b - c) for c in range(half)],
            range(1, n),
            True,
        )

    def inverse(product, result, tile):
        @pl.loop(0, half, step=2, unroll=True)
        def _(block):
            wide = jnp.concatenate([product[tile, block], product[tile, block + 1]], axis=1)
            high = wide.astype(jnp.bfloat16)
            low = (wide - high.astype(jnp.float32)).astype(jnp.bfloat16)
            both = dot(back_table[...], jnp.concatenate([high, high, low], axis=0))
            result[tile, block] = both[:, :chans].astype(jnp.bfloat16)
            result[tile, block + 1] = both[:, chans:].astype(jnp.bfloat16)

    def filter_spectra(tile):
        wait_for(recv_sem.at[FILTER, tile], filter_in.at[tile, pl.ds(0, n - 1)])
        taps[0] = jnp.zeros(taps.shape[1:], jnp.bfloat16)

        @pl.loop(0, n, unroll=True)
        def _(block):
            taps[block + 1] = filter_in[tile, block].astype(jnp.float32).T.astype(jnp.bfloat16)

        @pl.loop(0, n, step=2, unroll=True)
        def _(block):
            before, here, after = taps[block], taps[block + 1], taps[block + 2]
            pair = jnp.concatenate(
                [
                    jnp.concatenate([before, here], axis=0),
                    jnp.concatenate([here, after], axis=0),
                ],
                axis=1,
            )
            both = dot(window_table[...], jnp.concatenate([pair, pair], axis=0))
            spec_filter[tile, block] = both[:, :chans]
            spec_filter[tile, block + 1] = both[:, chans:]

    def send_results(kind, source_of, target, slot, tile):
        @pl.loop(0, half)
        def _(step):
            index = turn(step)
            start(
                source_of(index),
                target.at[:, cols(mine, tile)],
                near_first + index,
                send_sem.at[kind, tile],
                result_sem.at[slot, tile, mine],
            )

        target[:, cols(mine, tile)] = source_of(mine)[...]

    def narrow_results(tile):
        @pl.when(lower)
        def _():
            narrow_in[tile, place] = value_loc[:, cols(mine, tile)]

        @pl.when(jnp.logical_not(lower))
        def _():
            narrow_in[tile, place] = grad_loc[:, cols(mine, tile)]

        wait_for(recv_sem.at[NARROW, tile], narrow_in.at[tile, pl.ds(0, half - 1)])
        spectrum(narrow_in, tile, 0)
        multiply_near(product_narrow, tile, jnp.where(lower, 1.0, -1.0))
        inverse(product_narrow, narrow_out, tile)

        @pl.when(lower)
        def _():
            send_results(RESULT_NARROW, lambda index: narrow_out.at[tile, index], conv_in, 0, tile)

        @pl.when(jnp.logical_not(lower))
        def _():
            send_results(RESULT_NARROW, lambda index: narrow_out.at[tile, half - 1 - index], back_in, 1, tile)

    def wide_near(tile):
        @pl.when(lower)
        def _():
            wide_in[tile, mirror] = grad_loc[:, cols(mine, tile)]

        @pl.when(jnp.logical_not(lower))
        def _():
            wide_in[tile, me] = value_loc[:, cols(mine, tile)]

        wait_for(recv_sem.at[WIDE_NEAR, tile], wide_in.at[tile, pl.ds(0, half - 1)])
        tile_sums(tile)
        spectrum(wide_in, tile, half)
        multiply_near(product_wide, tile, jnp.where(lower, -1.0, 1.0))

    def wide_results(tile):
        wait_for(recv_sem.at[WIDE_FAR, tile], wide_in.at[tile, pl.ds(0, half)])
        spectrum(wide_in, tile, 0)
        multiply_far(product_wide, tile, jnp.where(lower, -1.0, 1.0))
        inverse(product_wide, wide_out, tile)

        @pl.when(lower)
        def _():
            send_results(RESULT_WIDE, lambda index: wide_out.at[tile, half - 1 - index], back_in, 1, tile)

        @pl.when(jnp.logical_not(lower))
        def _():
            send_results(RESULT_WIDE, lambda index: wide_out.at[tile, index], conv_in, 0, tile)

    def tile_sums(tile):
        @pl.loop(0, rows // 16, init_carry=jnp.zeros((16, chans), jnp.float32))
        def total(step, carry):
            at = pl.ds(pl.multiple_of(step * 16, 16), 16)
            for block in range(half):
                carry += narrow_in[tile, block, at, :].astype(jnp.float32) * wide_in[
                    tile, n - 1 - block, at, :
                ].astype(jnp.float32)
            return carry

        sums_out[tile] = jnp.sum(total, axis=0, keepdims=True) * (1.0 / math.sqrt(length))
        sums_in[me, tile] = sums_out[tile]

        @pl.loop(0, n)
        def _(device):
            start(
                sums_out.at[tile],
                sums_in.at[me, tile],
                device,
                sums_send_sem.at[tile],
                sums_sem.at[me, tile],
            )

    for stage in (filter_spectra, narrow_results, wide_near, wide_results):
        pl.loop(0, 2)(stage)

    def finish_conv(at):
        cot_rows = cot_loc[:, at].astype(jnp.float32)
        gate_rows = gate_loc[:, at].astype(jnp.float32)
        mixed = conv_in[:, at].astype(jnp.float32) + skip[:, at] * value_loc[:, at].astype(
            jnp.float32
        )
        output[:, at] = (gate_rows * mixed).astype(jnp.bfloat16)
        gate_grad[:, at] = (cot_rows * mixed).astype(jnp.bfloat16)

    def finish_back(at):
        grads = grad_loc[:, at].astype(jnp.float32)
        value_grad[:, at] = (back_in[:, at].astype(jnp.float32) + skip[:, at] * grads).astype(
            jnp.bfloat16
        )

    def take(slot, landing, finish, tile):
        @pl.loop(0, half)
        def _(step):
            index = lax.rem(mine + step, half)
            at = cols(index, tile)
            other(
                near_first + index,
                lambda: wait_for(result_sem.at[slot, tile, index], landing.at[:, at]),
            )
            finish(at)

    def take_sums():
        @pl.loop(0, n)
        def _(device):
            for tile in range(2):
                other(
                    device,
                    lambda tile=tile: wait_for(sums_sem.at[device, tile], sums_in.at[device, tile]),
                )

        for index in range(half):
            for tile in range(2):
                sums_table[2 * index + tile] = sums_in[index, tile] + sums_in[half + index, tile]
        gain[...] = sums_table[owner[me]]

    for narrow in (True, False):

        @pl.loop(0, 2)
        def _(tile, narrow=narrow):
            @pl.when(lower if narrow else jnp.logical_not(lower))
            def _():
                take(0, conv_in, finish_conv, tile)

            @pl.when(jnp.logical_not(lower) if narrow else lower)
            def _():
                take(1, back_in, finish_back, tile)

            if narrow:
                for kind, count in (
                    (FILTER, n - 1),
                    (NARROW, half - 1),
                    (WIDE_NEAR, half - 1),
                    (WIDE_FAR, half),
                    (RESULT_NARROW, half - 1),
                ):
                    wait_for(send_sem.at[kind, tile], wide_in.at[tile, pl.ds(0, count)])
                wait_for(sums_send_sem.at[tile], sums_table.at[pl.ds(0, n - 1)])
            else:
                wait_for(send_sem.at[RESULT_WIDE, tile], wide_in.at[tile, pl.ds(0, half - 1)])

        if narrow:
            take_sums()


def finish_kernel(
    output_loc, value_grad_loc, gate_grad_loc, gain_loc, output, value_grad, gate_grad, gain, sem
):
    copies = [
        pltpu.make_async_copy(source, target, sem.at[index])
        for index, (source, target) in enumerate(
            (
                (output_loc, output),
                (value_grad_loc, value_grad),
                (gate_grad_loc, gate_grad),
                (gain_loc, gain),
            )
        )
    ]
    for copy in copies:
        copy.start()
    for copy in copies:
        copy.wait()


def fused_body(value, gate, long_filter, skip_gain, cotangent, owner_map):
    n = lax.axis_size("seq")
    rows, group = value.shape
    chans = group // n
    tables = block_tables(rows)
    anywhere = pl.BlockSpec(memory_space=pltpu.HBM)
    vmem = pl.BlockSpec(memory_space=pltpu.VMEM)
    bf16, f32 = jnp.bfloat16, jnp.float32
    half = n // 2
    half_spec = pltpu.VMEM((2, half, 2 * rows, chans), f32)
    tokens = pltpu.VMEM((rows, group), bf16)
    tiles = pltpu.VMEM((2, n, rows, chans), bf16)
    half_tiles = pltpu.VMEM((2, half, rows, chans), bf16)
    local = pl.pallas_call(
        functools.partial(fused_kernel, n),
        out_shape=(tokens, tokens, tokens, pltpu.VMEM((1, chans), f32)),
        in_specs=[anywhere] * 9,
        out_specs=(vmem,) * 4,
        scratch_shapes=[
            *(pltpu.VMEM(table.shape, bf16) for table in tables),
            pltpu.VMEM((1, group), f32),
            pltpu.SMEM(owner_map.shape, jnp.int32),
            tokens,
            tokens,
            tokens,
            tokens,
            pltpu.VMEM((2, n, chans, rows), bf16),
            half_tiles,
            tiles,
            pltpu.VMEM((n + 1, rows, chans), bf16),
            pltpu.VMEM((2, n, 2 * rows, chans), f32),
            pltpu.VMEM((half, 2 * rows, chans), f32),
            half_spec,
            half_spec,
            half_tiles,
            half_tiles,
            tokens,
            tokens,
            pltpu.VMEM((2, 1, chans), f32),
            pltpu.VMEM((n, 2, 1, chans), f32),
            pltpu.VMEM((n, 1, chans), f32),
            pltpu.SemaphoreType.DMA((KINDS, 2)),
            pltpu.SemaphoreType.DMA((KINDS, 2)),
            pltpu.SemaphoreType.DMA((2, 2, half)),
            pltpu.SemaphoreType.DMA((2,)),
            pltpu.SemaphoreType.DMA((n, 2)),
            pltpu.SemaphoreType.DMA((10,)),
        ],
        compiler_params=pltpu.CompilerParams(
            collective_id=0,
            has_side_effects=True,
            vmem_limit_bytes=DEVICE_VMEM - 6 * rows * group - 2**16,
        ),
    )(
        value,
        long_filter,
        gate,
        cotangent,
        skip_gain.reshape(1, group),
        owner_map,
        *tables,
    )
    result = jax.ShapeDtypeStruct((rows, group), bf16)
    output, value_grad, gate_grad, gain = pl.pallas_call(
        finish_kernel,
        out_shape=(result, result, result, jax.ShapeDtypeStruct((1, chans), f32)),
        in_specs=[vmem] * 4,
        out_specs=(anywhere,) * 4,
        scratch_shapes=[pltpu.SemaphoreType.DMA((4,))],
        compiler_params=pltpu.CompilerParams(vmem_limit_bytes=2**20),
    )(*local)
    return (output, value_grad, gate_grad, gain.reshape(1, 1, chans))


def body(value, gate, long_filter, skip_gain, cotangent, owner_map):
    n = lax.axis_size("seq")
    rows, group = value.shape
    aligned = rows % LANES == 0 and group % (n * LANES) == 0 and n % 4 == 0
    needed = 64 * rows * group + 48 * rows * rows
    chosen = fused_body if aligned and needed <= DEVICE_VMEM // 2 else split_body
    return chosen(value, gate, long_filter, skip_gain, cotangent, owner_map)


def solution(mesh):
    in_specs = (
        P("seq", "chan"),
        P("seq", "chan"),
        P("chan", "seq"),
        P("chan"),
        P("seq", "chan"),
        P(),
    )
    out_specs = (P("seq", "chan"), P("seq", "chan"), P("seq", "chan"), P("chan", "seq", None))
    return jax.shard_map(body, mesh=mesh, in_specs=in_specs, out_specs=out_specs, check_vma=False)
```

```python
import functools
import math

import jax
import jax.numpy as jnp
import numpy as np
from jax import lax
from jax.experimental import pallas as pl
from jax.experimental.pallas import tpu as pltpu
from jax.sharding import PartitionSpec as P

HIGHEST = lax.Precision.HIGHEST


def dft_table(size):
    index = jnp.arange(size, dtype=jnp.int32)
    phase = index[:, None] * index[None, :] % size
    angle = 2.0 * math.pi / size * phase.astype(jnp.float32)
    return (jnp.cos(angle), jnp.sin(angle))


def make_tables(outer, inner):
    cos_outer, sin_outer = dft_table(outer)
    cos_inner, sin_inner = dft_table(inner)
    total = outer * inner
    phase = (
        jnp.arange(outer, dtype=jnp.int32)[:, None]
        * jnp.arange(inner, dtype=jnp.int32)[None, :]
        % total
    )
    angle = 2.0 * math.pi / total * phase.astype(jnp.float32)
    return (cos_outer, sin_outer, cos_inner, sin_inner, jnp.cos(angle), jnp.sin(angle))


def forward_dft(signal, tables):
    cos_outer, sin_outer, cos_inner, sin_inner, turn_cos, turn_sin = tables
    blocks = signal.shape[0]
    real_part = jnp.einsum("kn,ncb->ckb", cos_outer[:, :blocks], signal, precision=HIGHEST)
    imag_part = -jnp.einsum("kn,ncb->ckb", sin_outer[:, :blocks], signal, precision=HIGHEST)
    twisted_real = real_part * turn_cos + imag_part * turn_sin
    twisted_imag = imag_part * turn_cos - real_part * turn_sin
    spec_real = jnp.einsum("ckn,nm->ckm", twisted_real, cos_inner, precision=HIGHEST) + jnp.einsum(
        "ckn,nm->ckm", twisted_imag, sin_inner, precision=HIGHEST
    )
    spec_imag = jnp.einsum("ckn,nm->ckm", twisted_imag, cos_inner, precision=HIGHEST) - jnp.einsum(
        "ckn,nm->ckm", twisted_real, sin_inner, precision=HIGHEST
    )
    return (spec_real, spec_imag)


def inverse_dft(spec_real, spec_imag, tables, blocks):
    cos_outer, sin_outer, cos_inner, sin_inner, turn_cos, turn_sin = tables
    total = cos_outer.shape[0] * cos_inner.shape[0]
    inner_real = jnp.einsum("ckm,mn->ckn", spec_real, cos_inner, precision=HIGHEST) - jnp.einsum(
        "ckm,mn->ckn", spec_imag, sin_inner, precision=HIGHEST
    )
    inner_imag = jnp.einsum("ckm,mn->ckn", spec_real, sin_inner, precision=HIGHEST) + jnp.einsum(
        "ckm,mn->ckn", spec_imag, cos_inner, precision=HIGHEST
    )
    turned_real = inner_real * turn_cos - inner_imag * turn_sin
    turned_imag = inner_real * turn_sin + inner_imag * turn_cos
    result = jnp.einsum(
        "nk,ckb->ncb", cos_outer[:blocks, :], turned_real, precision=HIGHEST
    ) - jnp.einsum("nk,ckb->ncb", sin_outer[:blocks, :], turned_imag, precision=HIGHEST)
    return result / total


def causal_conv(sent_value, filter_spec, tables):
    value_real, value_imag = forward_dft(sent_value.astype(jnp.float32), tables)
    filter_real, filter_imag = filter_spec
    product_real = value_real * filter_real - value_imag * filter_imag
    product_imag = value_real * filter_imag + value_imag * filter_real
    return inverse_dft(product_real, product_imag, tables, sent_value.shape[0]).astype(jnp.bfloat16)


def transposed_conv(sent_grad, filter_spec, tables):
    grad_real, grad_imag = forward_dft(sent_grad.astype(jnp.float32), tables)
    filter_real, filter_imag = filter_spec
    product_real = grad_real * filter_real + grad_imag * filter_imag
    product_imag = grad_imag * filter_real - grad_real * filter_imag
    return inverse_dft(product_real, product_imag, tables, sent_grad.shape[0]).astype(jnp.bfloat16)


def split_body(value, gate, long_filter, skip_gain, cotangent, owner_map):
    blocks = lax.axis_size("seq")
    tok_rows = value.shape[0]
    group = value.shape[1]
    per_device = group // blocks
    value_rows = value.astype(jnp.float32)
    gate_rows = gate.astype(jnp.float32)
    grad_rows = (cotangent.astype(jnp.float32) * gate_rows).astype(jnp.bfloat16)
    value_major = value.T
    grad_major = grad_rows.T
    tables = make_tables(2 * blocks, tok_rows)
    value_split = value_major.reshape(blocks, per_device, tok_rows)
    filter_split = long_filter.reshape(blocks, per_device, tok_rows)
    grad_split = grad_major.reshape(blocks, per_device, tok_rows)
    sent_value, sent_filter = (
        lax.all_to_all(value_split, "seq", split_axis=0, concat_axis=0, tiled=True),
        lax.all_to_all(filter_split, "seq", split_axis=0, concat_axis=0, tiled=True),
    )
    filter_spec = forward_dft(sent_filter.astype(jnp.float32), tables)
    conv_back = lax.all_to_all(
        causal_conv(sent_value, filter_spec, tables), "seq", split_axis=0, concat_axis=0, tiled=True
    )
    sent_grad = lax.all_to_all(grad_split, "seq", split_axis=0, concat_axis=0, tiled=True)
    grad_back = lax.all_to_all(
        transposed_conv(sent_grad, filter_spec, tables),
        "seq",
        split_axis=0,
        concat_axis=0,
        tiled=True,
    )
    conv_rows = conv_back.reshape(group, tok_rows).T.astype(jnp.float32)
    mixed = conv_rows + skip_gain * value_rows
    output = (gate_rows * mixed).astype(jnp.bfloat16)
    gate_grad = (cotangent.astype(jnp.float32) * mixed).astype(jnp.bfloat16)
    back_rows = grad_back.reshape(group, tok_rows).T.astype(jnp.float32)
    grad_float = grad_rows.astype(jnp.float32)
    value_grad = (back_rows + skip_gain * grad_float).astype(jnp.bfloat16)
    scale = 1.0 / math.sqrt(tok_rows * blocks)
    local_sums = (
        jnp.sum(sent_value.astype(jnp.float32) * sent_grad.astype(jnp.float32), axis=(0, 2)) * scale
    )
    gathered = lax.all_gather(local_sums.reshape(1, per_device), "seq", axis=0, tiled=True)
    mine = owner_map[lax.axis_index("seq")]
    summed = lax.dynamic_slice_in_dim(gathered, mine, 1, 0)
    gain_grad = summed.reshape(1, 1, per_device)
    return (output, value_grad, gate_grad, gain_grad)


LANES = 128
DEVICE_VMEM = 67043328
FILTER, NARROW, WIDE_NEAR, WIDE_FAR, RESULT_NARROW, RESULT_WIDE, KINDS = range(7)
MESH = pl.DeviceIdType.MESH


def block_tables(rows):
    angle = math.pi / (2 * rows) * (2 * np.arange(rows, dtype=np.float64)[:, None] + 1)
    tokens = angle * np.arange(rows, dtype=np.float64)[None, :]
    window = angle * np.arange(-rows, rows, dtype=np.float64)[None, :]

    def parts(wide):
        high = wide.astype(jnp.bfloat16)
        return high, (wide - high.astype(np.float64)).astype(jnp.bfloat16)

    signal_high, signal_low = parts(np.concatenate([np.cos(tokens), -np.sin(tokens)]))
    window_high, window_low = parts(np.concatenate([np.cos(window), -np.sin(window)]))
    back = np.concatenate([np.cos(tokens), -np.sin(tokens)]).T / rows
    back_high, back_low = parts(back)
    return (
        np.concatenate([signal_high, signal_low], axis=1),
        np.concatenate([window_high, window_low], axis=1),
        np.concatenate([back_high, back_low, back_high], axis=1),
    )


def fused_kernel(
    n,
    value,
    filt,
    gate,
    cot,
    skip_any,
    owner_any,
    signal_any,
    window_any,
    back_any,
    output,
    value_grad,
    gate_grad,
    gain,
    signal_table,
    window_table,
    back_table,
    skip,
    owner,
    value_loc,
    gate_loc,
    cot_loc,
    grad_loc,
    filter_in,
    narrow_in,
    wide_in,
    taps,
    spec_filter,
    spec_signal,
    product_narrow,
    product_wide,
    narrow_out,
    wide_out,
    conv_in,
    back_in,
    sums_out,
    sums_in,
    sums_table,
    send_sem,
    recv_sem,
    result_sem,
    sums_send_sem,
    sums_sem,
    local_sem,
):
    me = lax.axis_index("seq")
    half = n // 2
    rows, group = value.shape
    chans = group // n
    length = rows * n
    lower = me < half
    mirror = n - 1 - me
    mine = lax.rem(me, half)
    place = jnp.where(lower, me, mirror)
    near_first = jnp.where(lower, 0, half)

    def cols(index, tile):
        return pl.ds(pl.multiple_of((2 * index + tile) * chans, chans), chans)

    def other(device, action):
        @pl.when(device != me)
        def _():
            action()

    def start(source, target, device, sent, arrival):
        def action():
            pltpu.make_async_remote_copy(
                src_ref=source,
                dst_ref=target,
                send_sem=sent,
                recv_sem=arrival,
                device_id={"seq": device},
                device_id_type=MESH,
            ).start()

        other(device, action)

    def wait_for(semaphore, blocks):
        pltpu.make_async_copy(blocks, blocks, semaphore).wait()

    barrier = pltpu.get_barrier_semaphore()

    @pl.loop(0, n)
    def _(device):
        def greet():
            pl.semaphore_signal(barrier, inc=1, device_id={"seq": device}, device_id_type=MESH)

        other(device, greet)

    local = [
        pltpu.make_async_copy(gate, gate_loc, local_sem.at[0]),
        pltpu.make_async_copy(cot, cot_loc, local_sem.at[1]),
        pltpu.make_async_copy(value, value_loc, local_sem.at[2]),
        pltpu.make_async_copy(signal_any, signal_table, local_sem.at[3]),
        pltpu.make_async_copy(window_any, window_table, local_sem.at[4]),
        pltpu.make_async_copy(back_any, back_table, local_sem.at[5]),
        pltpu.make_async_copy(skip_any, skip, local_sem.at[6]),
        pltpu.make_async_copy(owner_any, owner, local_sem.at[7]),
        pltpu.make_async_copy(filt.at[cols(mine, 0), :], filter_in.at[0, me], local_sem.at[8]),
        pltpu.make_async_copy(filt.at[cols(mine, 1), :], filter_in.at[1, me], local_sem.at[9]),
    ]
    for copy in local:
        copy.start()
    pl.semaphore_wait(barrier, n - 1)

    def turn(step):
        away = jnp.where(step < half // 2, half - 1 - 2 * step, 2 * (half - 1 - step))
        return lax.rem(mine // 2 + away // 2, half // 2) * 2 + lax.rem(mine + away, 2)

    def send(kind, source_of, target, tile, far):
        first = half - near_first if far else near_first

        @pl.loop(0, half)
        def _(step):
            index = turn(step)
            start(
                source_of(index),
                target,
                first + index,
                send_sem.at[kind, tile],
                recv_sem.at[kind, tile],
            )

    def send_filter(tile, far):
        send(FILTER, lambda i: filt.at[cols(i, tile), :], filter_in.at[tile, me], tile, far)

    def send_value(tile, far, near):
        def source(index):
            return value.at[:, cols(index, tile)]

        @pl.when(lower)
        def _():
            if far:
                send(WIDE_FAR, source, wide_in.at[tile, me], tile, True)
            if near:
                send(NARROW, source, narrow_in.at[tile, me], tile, False)

        if near:

            @pl.when(jnp.logical_not(lower))
            def _():
                send(WIDE_NEAR, source, wide_in.at[tile, me], tile, False)

    def send_grad(tile, far, near):
        def source(index):
            return grad_loc.at[:, cols(index, tile)]

        @pl.when(jnp.logical_not(lower))
        def _():
            if far:
                send(WIDE_FAR, source, wide_in.at[tile, mirror], tile, True)
            if near:
                send(NARROW, source, narrow_in.at[tile, mirror], tile, False)

        if near:

            @pl.when(lower)
            def _():
                send(WIDE_NEAR, source, wide_in.at[tile, mirror], tile, False)

    def make_grads():
        local[0].wait()
        local[1].wait()

        @pl.loop(0, rows // 16)
        def _(step):
            at = pl.ds(pl.multiple_of(step * 16, 16), 16)
            grads = cot_loc[at, :].astype(jnp.float32) * gate_loc[at, :].astype(jnp.float32)
            grad_loc[at, :] = grads.astype(jnp.bfloat16)

    @pl.loop(0, 2)
    def _(tile):
        send_filter(tile, True)
        send_filter(tile, False)

    make_grads()

    @pl.loop(0, 2)
    def _(tile):
        send_value(tile, False, True)
        send_grad(tile, False, True)

    @pl.loop(0, 2)
    def _(tile):
        send_value(tile, True, False)
        send_grad(tile, True, False)
    for copy in local[2:]:
        copy.wait()

    def dot(left, right):
        return jnp.dot(left, right, preferred_element_type=jnp.float32)

    def spectrum(signal, tile, first):
        @pl.loop(0, half, step=2, unroll=True)
        def _(block):
            pair = jnp.concatenate(
                [signal[tile, first + block], signal[tile, first + block + 1]], axis=1
            )
            both = dot(signal_table[...], jnp.concatenate([pair, pair], axis=0))
            spec_signal[block] = both[:, :chans]
            spec_signal[block + 1] = both[:, chans:]

    def multiply(result, tile, sign, pairs, windows, adds):
        @pl.loop(0, rows // 8)
        def _(step):
            real = pl.ds(pl.multiple_of(step * 8, 8), 8)
            imag = pl.ds(pl.multiple_of(rows + step * 8, 8), 8)
            signal_real = [spec_signal[c, real, :] for c in range(half)]
            signal_imag = [spec_signal[c, imag, :] for c in range(half)]
            filter_real = {d: spec_filter[tile, d, real, :] for d in windows}
            filter_imag = {d: spec_filter[tile, d, imag, :] * sign for d in windows}
            for block in range(half):
                total_real = result[tile, block, real, :] if adds else None
                total_imag = result[tile, block, imag, :] if adds else None
                for c, d in pairs(block):
                    with_real, with_imag = filter_real[d], filter_imag[d]
                    term_real = signal_real[c] * with_real - signal_imag[c] * with_imag
                    term_imag = signal_imag[c] * with_real + signal_real[c] * with_imag
                    total_real = term_real if total_real is None else total_real + term_real
                    total_imag = term_imag if total_imag is None else total_imag + term_imag
                result[tile, block, real, :] = total_real
                result[tile, block, imag, :] = total_imag

    def multiply_near(result, tile, sign):
        multiply(
            result, tile, sign, lambda b: [(c, b - c) for c in range(b + 1)], range(half), False
        )

    def multiply_far(result, tile, sign):
        multiply(
            result,
            tile,
            sign,
            lambda b: [(c, half + b - c) for c in range(half)],
            range(1, n),
            True,
        )

    def inverse(product, result, tile):
        @pl.loop(0, half, step=2, unroll=True)
        def _(block):
            wide = jnp.concatenate([product[tile, block], product[tile, block + 1]], axis=1)
            high = wide.astype(jnp.bfloat16)
            low = (wide - high.astype(jnp.float32)).astype(jnp.bfloat16)
            both = dot(back_table[...], jnp.concatenate([high, high, low], axis=0))
            result[tile, block] = both[:, :chans].astype(jnp.bfloat16)
            result[tile, block + 1] = both[:, chans:].astype(jnp.bfloat16)

    def filter_spectra(tile):
        wait_for(recv_sem.at[FILTER, tile], filter_in.at[tile, pl.ds(0, n - 1)])
        taps[0] = jnp.zeros(taps.shape[1:], jnp.bfloat16)

        @pl.loop(0, n, unroll=True)
        def _(block):
            taps[block + 1] = filter_in[tile, block].astype(jnp.float32).T.astype(jnp.bfloat16)

        @pl.loop(0, n, step=2, unroll=True)
        def _(block):
            before, here, after = taps[block], taps[block + 1], taps[block + 2]
            pair = jnp.concatenate(
                [
                    jnp.concatenate([before, here], axis=0),
                    jnp.concatenate([here, after], axis=0),
                ],
                axis=1,
            )
            both = dot(window_table[...], jnp.concatenate([pair, pair], axis=0))
            spec_filter[tile, block] = both[:, :chans]
            spec_filter[tile, block + 1] = both[:, chans:]

    def send_results(kind, source_of, target, slot, tile):
        @pl.loop(0, half)
        def _(step):
            index = turn(step)
            start(
                source_of(index),
                target.at[:, cols(mine, tile)],
                near_first + index,
                send_sem.at[kind, tile],
                result_sem.at[slot, tile, mine],
            )

        target[:, cols(mine, tile)] = source_of(mine)[...]

    def narrow_results(tile):
        @pl.when(lower)
        def _():
            narrow_in[tile, place] = value_loc[:, cols(mine, tile)]

        @pl.when(jnp.logical_not(lower))
        def _():
            narrow_in[tile, place] = grad_loc[:, cols(mine, tile)]

        wait_for(recv_sem.at[NARROW, tile], narrow_in.at[tile, pl.ds(0, half - 1)])
        spectrum(narrow_in, tile, 0)
        multiply_near(product_narrow, tile, jnp.where(lower, 1.0, -1.0))
        inverse(product_narrow, narrow_out, tile)

        @pl.when(lower)
        def _():
            send_results(RESULT_NARROW, lambda index: narrow_out.at[tile, index], conv_in, 0, tile)

        @pl.when(jnp.logical_not(lower))
        def _():
            send_results(RESULT_NARROW, lambda index: narrow_out.at[tile, half - 1 - index], back_in, 1, tile)

    def wide_near(tile):
        @pl.when(lower)
        def _():
            wide_in[tile, mirror] = grad_loc[:, cols(mine, tile)]

        @pl.when(jnp.logical_not(lower))
        def _():
            wide_in[tile, me] = value_loc[:, cols(mine, tile)]

        wait_for(recv_sem.at[WIDE_NEAR, tile], wide_in.at[tile, pl.ds(0, half - 1)])
        tile_sums(tile)
        spectrum(wide_in, tile, half)
        multiply_near(product_wide, tile, jnp.where(lower, -1.0, 1.0))

    def wide_results(tile):
        wait_for(recv_sem.at[WIDE_FAR, tile], wide_in.at[tile, pl.ds(0, half)])
        spectrum(wide_in, tile, 0)
        multiply_far(product_wide, tile, jnp.where(lower, -1.0, 1.0))
        inverse(product_wide, wide_out, tile)

        @pl.when(lower)
        def _():
            send_results(RESULT_WIDE, lambda index: wide_out.at[tile, half - 1 - index], back_in, 1, tile)

        @pl.when(jnp.logical_not(lower))
        def _():
            send_results(RESULT_WIDE, lambda index: wide_out.at[tile, index], conv_in, 0, tile)

    def tile_sums(tile):
        @pl.loop(0, rows // 16, init_carry=jnp.zeros((16, chans), jnp.float32))
        def total(step, carry):
            at = pl.ds(pl.multiple_of(step * 16, 16), 16)
            for block in range(half):
                carry += narrow_in[tile, block, at, :].astype(jnp.float32) * wide_in[
                    tile, n - 1 - block, at, :
                ].astype(jnp.float32)
            return carry

        sums_out[tile] = jnp.sum(total, axis=0, keepdims=True) * (1.0 / math.sqrt(length))
        sums_in[me, tile] = sums_out[tile]

        @pl.when(tile == 1)
        def _():
            @pl.loop(0, n)
            def _(device):
                start(
                    sums_out, sums_in.at[me], device, sums_send_sem.at[0], sums_sem.at[me]
                )

    for stage in (filter_spectra, narrow_results, wide_near, wide_results):
        pl.loop(0, 2)(stage)

    def finish_conv(at):
        cot_rows = cot_loc[:, at].astype(jnp.float32)
        gate_rows = gate_loc[:, at].astype(jnp.float32)
        mixed = conv_in[:, at].astype(jnp.float32) + skip[:, at] * value_loc[:, at].astype(
            jnp.float32
        )
        output[:, at] = (gate_rows * mixed).astype(jnp.bfloat16)
        gate_grad[:, at] = (cot_rows * mixed).astype(jnp.bfloat16)

    def finish_back(at):
        grads = grad_loc[:, at].astype(jnp.float32)
        value_grad[:, at] = (back_in[:, at].astype(jnp.float32) + skip[:, at] * grads).astype(
            jnp.bfloat16
        )

    def take(slot, landing, finish, tile):
        @pl.loop(0, half)
        def _(step):
            index = lax.rem(mine + step, half)
            at = cols(index, tile)
            other(
                near_first + index,
                lambda: wait_for(result_sem.at[slot, tile, index], landing.at[:, at]),
            )
            finish(at)

    def take_sums():
        @pl.loop(0, n)
        def _(device):
            other(device, lambda: wait_for(sums_sem.at[device], sums_in.at[device]))

        for index in range(half):
            for tile in range(2):
                sums_table[2 * index + tile] = sums_in[index, tile] + sums_in[half + index, tile]
        gain[...] = sums_table[owner[me]]

    for narrow in (True, False):

        @pl.loop(0, 2)
        def _(tile, narrow=narrow):
            @pl.when(lower if narrow else jnp.logical_not(lower))
            def _():
                take(0, conv_in, finish_conv, tile)

            @pl.when(jnp.logical_not(lower) if narrow else lower)
            def _():
                take(1, back_in, finish_back, tile)

            if narrow:
                for kind, count in (
                    (FILTER, n - 1),
                    (NARROW, half - 1),
                    (WIDE_NEAR, half - 1),
                    (WIDE_FAR, half),
                    (RESULT_NARROW, half - 1),
                ):
                    wait_for(send_sem.at[kind, tile], wide_in.at[tile, pl.ds(0, count)])
            else:
                wait_for(send_sem.at[RESULT_WIDE, tile], wide_in.at[tile, pl.ds(0, half - 1)])

        if narrow:
            take_sums()
            wait_for(sums_send_sem.at[0], sums_in.at[pl.ds(0, n - 1)])


def finish_kernel(
    output_loc, value_grad_loc, gate_grad_loc, gain_loc, output, value_grad, gate_grad, gain, sem
):
    copies = [
        pltpu.make_async_copy(source, target, sem.at[index])
        for index, (source, target) in enumerate(
            (
                (output_loc, output),
                (value_grad_loc, value_grad),
                (gate_grad_loc, gate_grad),
                (gain_loc, gain),
            )
        )
    ]
    for copy in copies:
        copy.start()
    for copy in copies:
        copy.wait()


def fused_body(value, gate, long_filter, skip_gain, cotangent, owner_map):
    n = lax.axis_size("seq")
    rows, group = value.shape
    chans = group // n
    tables = block_tables(rows)
    anywhere = pl.BlockSpec(memory_space=pltpu.HBM)
    vmem = pl.BlockSpec(memory_space=pltpu.VMEM)
    bf16, f32 = jnp.bfloat16, jnp.float32
    half = n // 2
    half_spec = pltpu.VMEM((2, half, 2 * rows, chans), f32)
    tokens = pltpu.VMEM((rows, group), bf16)
    tiles = pltpu.VMEM((2, n, rows, chans), bf16)
    half_tiles = pltpu.VMEM((2, half, rows, chans), bf16)
    local = pl.pallas_call(
        functools.partial(fused_kernel, n),
        out_shape=(tokens, tokens, tokens, pltpu.VMEM((1, chans), f32)),
        in_specs=[anywhere] * 9,
        out_specs=(vmem,) * 4,
        scratch_shapes=[
            *(pltpu.VMEM(table.shape, bf16) for table in tables),
            pltpu.VMEM((1, group), f32),
            pltpu.SMEM(owner_map.shape, jnp.int32),
            tokens,
            tokens,
            tokens,
            tokens,
            pltpu.VMEM((2, n, chans, rows), bf16),
            half_tiles,
            tiles,
            pltpu.VMEM((n + 1, rows, chans), bf16),
            pltpu.VMEM((2, n, 2 * rows, chans), f32),
            pltpu.VMEM((half, 2 * rows, chans), f32),
            half_spec,
            half_spec,
            half_tiles,
            half_tiles,
            tokens,
            tokens,
            pltpu.VMEM((2, 1, chans), f32),
            pltpu.VMEM((n, 2, 1, chans), f32),
            pltpu.VMEM((n, 1, chans), f32),
            pltpu.SemaphoreType.DMA((KINDS, 2)),
            pltpu.SemaphoreType.DMA((KINDS, 2)),
            pltpu.SemaphoreType.DMA((2, 2, half)),
            pltpu.SemaphoreType.DMA((1,)),
            pltpu.SemaphoreType.DMA((n,)),
            pltpu.SemaphoreType.DMA((10,)),
        ],
        compiler_params=pltpu.CompilerParams(
            collective_id=0,
            has_side_effects=True,
            vmem_limit_bytes=DEVICE_VMEM - 6 * rows * group - 2**16,
        ),
    )(
        value,
        long_filter,
        gate,
        cotangent,
        skip_gain.reshape(1, group),
        owner_map,
        *tables,
    )
    result = jax.ShapeDtypeStruct((rows, group), bf16)
    output, value_grad, gate_grad, gain = pl.pallas_call(
        finish_kernel,
        out_shape=(result, result, result, jax.ShapeDtypeStruct((1, chans), f32)),
        in_specs=[vmem] * 4,
        out_specs=(anywhere,) * 4,
        scratch_shapes=[pltpu.SemaphoreType.DMA((4,))],
        compiler_params=pltpu.CompilerParams(vmem_limit_bytes=2**20),
    )(*local)
    return (output, value_grad, gate_grad, gain.reshape(1, 1, chans))


def body(value, gate, long_filter, skip_gain, cotangent, owner_map):
    n = lax.axis_size("seq")
    rows, group = value.shape
    aligned = rows % LANES == 0 and group % (n * LANES) == 0 and n % 4 == 0
    needed = 64 * rows * group + 48 * rows * rows
    chosen = fused_body if aligned and needed <= DEVICE_VMEM // 2 else split_body
    return chosen(value, gate, long_filter, skip_gain, cotangent, owner_map)


def solution(mesh):
    in_specs = (
        P("seq", "chan"),
        P("seq", "chan"),
        P("chan", "seq"),
        P("chan"),
        P("seq", "chan"),
        P(),
    )
    out_specs = (P("seq", "chan"), P("seq", "chan"), P("seq", "chan"), P("chan", "seq", None))
    return jax.shard_map(body, mesh=mesh, in_specs=in_specs, out_specs=out_specs, check_vma=False)
```

```python
import functools
import math

import jax
import jax.numpy as jnp
import numpy as np
from jax import lax
from jax.experimental import pallas as pl
from jax.experimental.pallas import tpu as pltpu
from jax.sharding import PartitionSpec as P

HIGHEST = lax.Precision.HIGHEST


def dft_table(size):
    index = jnp.arange(size, dtype=jnp.int32)
    phase = index[:, None] * index[None, :] % size
    angle = 2.0 * math.pi / size * phase.astype(jnp.float32)
    return (jnp.cos(angle), jnp.sin(angle))


def make_tables(outer, inner):
    cos_outer, sin_outer = dft_table(outer)
    cos_inner, sin_inner = dft_table(inner)
    total = outer * inner
    phase = (
        jnp.arange(outer, dtype=jnp.int32)[:, None]
        * jnp.arange(inner, dtype=jnp.int32)[None, :]
        % total
    )
    angle = 2.0 * math.pi / total * phase.astype(jnp.float32)
    return (cos_outer, sin_outer, cos_inner, sin_inner, jnp.cos(angle), jnp.sin(angle))


def forward_dft(signal, tables):
    cos_outer, sin_outer, cos_inner, sin_inner, turn_cos, turn_sin = tables
    blocks = signal.shape[0]
    real_part = jnp.einsum("kn,ncb->ckb", cos_outer[:, :blocks], signal, precision=HIGHEST)
    imag_part = -jnp.einsum("kn,ncb->ckb", sin_outer[:, :blocks], signal, precision=HIGHEST)
    twisted_real = real_part * turn_cos + imag_part * turn_sin
    twisted_imag = imag_part * turn_cos - real_part * turn_sin
    spec_real = jnp.einsum("ckn,nm->ckm", twisted_real, cos_inner, precision=HIGHEST) + jnp.einsum(
        "ckn,nm->ckm", twisted_imag, sin_inner, precision=HIGHEST
    )
    spec_imag = jnp.einsum("ckn,nm->ckm", twisted_imag, cos_inner, precision=HIGHEST) - jnp.einsum(
        "ckn,nm->ckm", twisted_real, sin_inner, precision=HIGHEST
    )
    return (spec_real, spec_imag)


def inverse_dft(spec_real, spec_imag, tables, blocks):
    cos_outer, sin_outer, cos_inner, sin_inner, turn_cos, turn_sin = tables
    total = cos_outer.shape[0] * cos_inner.shape[0]
    inner_real = jnp.einsum("ckm,mn->ckn", spec_real, cos_inner, precision=HIGHEST) - jnp.einsum(
        "ckm,mn->ckn", spec_imag, sin_inner, precision=HIGHEST
    )
    inner_imag = jnp.einsum("ckm,mn->ckn", spec_real, sin_inner, precision=HIGHEST) + jnp.einsum(
        "ckm,mn->ckn", spec_imag, cos_inner, precision=HIGHEST
    )
    turned_real = inner_real * turn_cos - inner_imag * turn_sin
    turned_imag = inner_real * turn_sin + inner_imag * turn_cos
    result = jnp.einsum(
        "nk,ckb->ncb", cos_outer[:blocks, :], turned_real, precision=HIGHEST
    ) - jnp.einsum("nk,ckb->ncb", sin_outer[:blocks, :], turned_imag, precision=HIGHEST)
    return result / total


def causal_conv(sent_value, filter_spec, tables):
    value_real, value_imag = forward_dft(sent_value.astype(jnp.float32), tables)
    filter_real, filter_imag = filter_spec
    product_real = value_real * filter_real - value_imag * filter_imag
    product_imag = value_real * filter_imag + value_imag * filter_real
    return inverse_dft(product_real, product_imag, tables, sent_value.shape[0]).astype(jnp.bfloat16)


def transposed_conv(sent_grad, filter_spec, tables):
    grad_real, grad_imag = forward_dft(sent_grad.astype(jnp.float32), tables)
    filter_real, filter_imag = filter_spec
    product_real = grad_real * filter_real + grad_imag * filter_imag
    product_imag = grad_imag * filter_real - grad_real * filter_imag
    return inverse_dft(product_real, product_imag, tables, sent_grad.shape[0]).astype(jnp.bfloat16)


def split_body(value, gate, long_filter, skip_gain, cotangent, owner_map):
    blocks = lax.axis_size("seq")
    tok_rows = value.shape[0]
    group = value.shape[1]
    per_device = group // blocks
    value_rows = value.astype(jnp.float32)
    gate_rows = gate.astype(jnp.float32)
    grad_rows = (cotangent.astype(jnp.float32) * gate_rows).astype(jnp.bfloat16)
    value_major = value.T
    grad_major = grad_rows.T
    tables = make_tables(2 * blocks, tok_rows)
    value_split = value_major.reshape(blocks, per_device, tok_rows)
    filter_split = long_filter.reshape(blocks, per_device, tok_rows)
    grad_split = grad_major.reshape(blocks, per_device, tok_rows)
    sent_value, sent_filter = (
        lax.all_to_all(value_split, "seq", split_axis=0, concat_axis=0, tiled=True),
        lax.all_to_all(filter_split, "seq", split_axis=0, concat_axis=0, tiled=True),
    )
    filter_spec = forward_dft(sent_filter.astype(jnp.float32), tables)
    conv_back = lax.all_to_all(
        causal_conv(sent_value, filter_spec, tables), "seq", split_axis=0, concat_axis=0, tiled=True
    )
    sent_grad = lax.all_to_all(grad_split, "seq", split_axis=0, concat_axis=0, tiled=True)
    grad_back = lax.all_to_all(
        transposed_conv(sent_grad, filter_spec, tables),
        "seq",
        split_axis=0,
        concat_axis=0,
        tiled=True,
    )
    conv_rows = conv_back.reshape(group, tok_rows).T.astype(jnp.float32)
    mixed = conv_rows + skip_gain * value_rows
    output = (gate_rows * mixed).astype(jnp.bfloat16)
    gate_grad = (cotangent.astype(jnp.float32) * mixed).astype(jnp.bfloat16)
    back_rows = grad_back.reshape(group, tok_rows).T.astype(jnp.float32)
    grad_float = grad_rows.astype(jnp.float32)
    value_grad = (back_rows + skip_gain * grad_float).astype(jnp.bfloat16)
    scale = 1.0 / math.sqrt(tok_rows * blocks)
    local_sums = (
        jnp.sum(sent_value.astype(jnp.float32) * sent_grad.astype(jnp.float32), axis=(0, 2)) * scale
    )
    gathered = lax.all_gather(local_sums.reshape(1, per_device), "seq", axis=0, tiled=True)
    mine = owner_map[lax.axis_index("seq")]
    summed = lax.dynamic_slice_in_dim(gathered, mine, 1, 0)
    gain_grad = summed.reshape(1, 1, per_device)
    return (output, value_grad, gate_grad, gain_grad)


LANES = 128
DEVICE_VMEM = 67043328
FILTER, NARROW, WIDE_NEAR, WIDE_FAR, RESULT_NARROW, RESULT_WIDE, KINDS = range(7)
MESH = pl.DeviceIdType.MESH


def block_tables(rows):
    angle = math.pi / (2 * rows) * (2 * np.arange(rows, dtype=np.float64)[:, None] + 1)
    tokens = angle * np.arange(rows, dtype=np.float64)[None, :]
    window = angle * np.arange(-rows, rows, dtype=np.float64)[None, :]

    def parts(wide):
        high = wide.astype(jnp.bfloat16)
        return high, (wide - high.astype(np.float64)).astype(jnp.bfloat16)

    signal_high, signal_low = parts(np.concatenate([np.cos(tokens), -np.sin(tokens)]))
    window_high, window_low = parts(np.concatenate([np.cos(window), -np.sin(window)]))
    back = np.concatenate([np.cos(tokens), -np.sin(tokens)]).T / rows
    back_high, back_low = parts(back)
    return (
        np.concatenate([signal_high, signal_low], axis=1),
        np.concatenate([window_high, window_low], axis=1),
        np.concatenate([back_high, back_low, back_high], axis=1),
    )


def fused_kernel(
    n,
    value,
    filt,
    gate,
    cot,
    skip_any,
    owner_any,
    signal_any,
    window_any,
    back_any,
    output,
    value_grad,
    gate_grad,
    gain,
    signal_table,
    window_table,
    back_table,
    skip,
    owner,
    value_loc,
    gate_loc,
    cot_loc,
    grad_loc,
    filter_in,
    narrow_in,
    wide_in,
    taps,
    spec_filter,
    spec_signal,
    product_narrow,
    product_wide,
    narrow_out,
    wide_out,
    conv_in,
    back_in,
    sums_out,
    sums_in,
    sums_table,
    send_sem,
    recv_sem,
    result_sem,
    sums_send_sem,
    sums_sem,
    local_sem,
):
    me = lax.axis_index("seq")
    half = n // 2
    rows, group = value.shape
    chans = group // n
    length = rows * n
    lower = me < half
    mirror = n - 1 - me
    mine = lax.rem(me, half)
    place = jnp.where(lower, me, mirror)
    near_first = jnp.where(lower, 0, half)

    def cols(index, tile):
        return pl.ds(pl.multiple_of((2 * index + tile) * chans, chans), chans)

    def other(device, action):
        @pl.when(device != me)
        def _():
            action()

    def start(source, target, device, sent, arrival):
        def action():
            pltpu.make_async_remote_copy(
                src_ref=source,
                dst_ref=target,
                send_sem=sent,
                recv_sem=arrival,
                device_id={"seq": device},
                device_id_type=MESH,
            ).start()

        other(device, action)

    def wait_for(semaphore, blocks):
        pltpu.make_async_copy(blocks, blocks, semaphore).wait()

    barrier = pltpu.get_barrier_semaphore()

    @pl.loop(0, n)
    def _(device):
        def greet():
            pl.semaphore_signal(barrier, inc=1, device_id={"seq": device}, device_id_type=MESH)

        other(device, greet)

    local = [
        pltpu.make_async_copy(gate, gate_loc, local_sem.at[0]),
        pltpu.make_async_copy(cot, cot_loc, local_sem.at[1]),
        pltpu.make_async_copy(value, value_loc, local_sem.at[2]),
        pltpu.make_async_copy(signal_any, signal_table, local_sem.at[3]),
        pltpu.make_async_copy(window_any, window_table, local_sem.at[4]),
        pltpu.make_async_copy(back_any, back_table, local_sem.at[5]),
        pltpu.make_async_copy(skip_any, skip, local_sem.at[6]),
        pltpu.make_async_copy(owner_any, owner, local_sem.at[7]),
        pltpu.make_async_copy(filt.at[cols(mine, 0), :], filter_in.at[0, me], local_sem.at[8]),
        pltpu.make_async_copy(filt.at[cols(mine, 1), :], filter_in.at[1, me], local_sem.at[9]),
    ]
    for copy in local:
        copy.start()
    pl.semaphore_wait(barrier, n - 1)

    def turn(step):
        away = jnp.where(step < half // 2, half - 1 - 2 * step, 2 * (half - 1 - step))
        return lax.rem(mine // 2 + away // 2, half // 2) * 2 + lax.rem(mine + away, 2)

    def send(kind, source_of, target, tile, far):
        first = half - near_first if far else near_first

        @pl.loop(0, half)
        def _(step):
            index = turn(step)
            start(
                source_of(index),
                target,
                first + index,
                send_sem.at[kind, tile],
                recv_sem.at[kind, tile],
            )

    def send_filter(tile, far):
        send(FILTER, lambda i: filt.at[cols(i, tile), :], filter_in.at[tile, me], tile, far)

    def send_value(tile, far, near):
        def source(index):
            return value_loc.at[:, cols(index, tile)]

        @pl.when(lower)
        def _():
            if far:
                send(WIDE_FAR, source, wide_in.at[tile, me], tile, True)
            if near:
                send(NARROW, source, narrow_in.at[tile, me], tile, False)

        if near:

            @pl.when(jnp.logical_not(lower))
            def _():
                send(WIDE_NEAR, source, wide_in.at[tile, me], tile, False)

    def send_grad(tile, far, near):
        def source(index):
            return grad_loc.at[:, cols(index, tile)]

        @pl.when(jnp.logical_not(lower))
        def _():
            if far:
                send(WIDE_FAR, source, wide_in.at[tile, mirror], tile, True)
            if near:
                send(NARROW, source, narrow_in.at[tile, mirror], tile, False)

        if near:

            @pl.when(lower)
            def _():
                send(WIDE_NEAR, source, wide_in.at[tile, mirror], tile, False)

    def make_grads():
        for copy in local[:3]:
            copy.wait()

        @pl.loop(0, rows // 16)
        def _(step):
            at = pl.ds(pl.multiple_of(step * 16, 16), 16)
            grads = cot_loc[at, :].astype(jnp.float32) * gate_loc[at, :].astype(jnp.float32)
            grad_loc[at, :] = grads.astype(jnp.bfloat16)

    @pl.loop(0, 2)
    def _(tile):
        send_filter(tile, True)
        send_filter(tile, False)

    make_grads()

    @pl.loop(0, 2)
    def _(tile):
        send_value(tile, False, True)
        send_grad(tile, False, True)

    @pl.loop(0, 2)
    def _(tile):
        send_value(tile, True, False)
        send_grad(tile, True, False)
    for copy in local[3:]:
        copy.wait()

    def dot(left, right):
        return jnp.dot(left, right, preferred_element_type=jnp.float32)

    def spectrum(signal, tile, first):
        @pl.loop(0, half, step=2, unroll=True)
        def _(block):
            pair = jnp.concatenate(
                [signal[tile, first + block], signal[tile, first + block + 1]], axis=1
            )
            both = dot(signal_table[...], jnp.concatenate([pair, pair], axis=0))
            spec_signal[block] = both[:, :chans]
            spec_signal[block + 1] = both[:, chans:]

    def multiply(result, tile, sign, pairs, windows, adds):
        @pl.loop(0, rows // 8)
        def _(step):
            real = pl.ds(pl.multiple_of(step * 8, 8), 8)
            imag = pl.ds(pl.multiple_of(rows + step * 8, 8), 8)
            signal_real = [spec_signal[c, real, :] for c in range(half)]
            signal_imag = [spec_signal[c, imag, :] for c in range(half)]
            filter_real = {d: spec_filter[tile, d, real, :] for d in windows}
            filter_imag = {d: spec_filter[tile, d, imag, :] * sign for d in windows}
            for block in range(half):
                total_real = result[tile, block, real, :] if adds else None
                total_imag = result[tile, block, imag, :] if adds else None
                for c, d in pairs(block):
                    with_real, with_imag = filter_real[d], filter_imag[d]
                    term_real = signal_real[c] * with_real - signal_imag[c] * with_imag
                    term_imag = signal_imag[c] * with_real + signal_real[c] * with_imag
                    total_real = term_real if total_real is None else total_real + term_real
                    total_imag = term_imag if total_imag is None else total_imag + term_imag
                result[tile, block, real, :] = total_real
                result[tile, block, imag, :] = total_imag

    def multiply_near(result, tile, sign):
        multiply(
            result, tile, sign, lambda b: [(c, b - c) for c in range(b + 1)], range(half), False
        )

    def multiply_far(result, tile, sign):
        multiply(
            result,
            tile,
            sign,
            lambda b: [(c, half + b - c) for c in range(half)],
            range(1, n),
            True,
        )

    def inverse(product, result, tile):
        @pl.loop(0, half, step=2, unroll=True)
        def _(block):
            wide = jnp.concatenate([product[tile, block], product[tile, block + 1]], axis=1)
            high = wide.astype(jnp.bfloat16)
            low = (wide - high.astype(jnp.float32)).astype(jnp.bfloat16)
            both = dot(back_table[...], jnp.concatenate([high, high, low], axis=0))
            result[tile, block] = both[:, :chans].astype(jnp.bfloat16)
            result[tile, block + 1] = both[:, chans:].astype(jnp.bfloat16)

    def filter_spectra(tile):
        wait_for(recv_sem.at[FILTER, tile], filter_in.at[tile, pl.ds(0, n - 1)])
        taps[0] = jnp.zeros(taps.shape[1:], jnp.bfloat16)

        @pl.loop(0, n, unroll=True)
        def _(block):
            taps[block + 1] = filter_in[tile, block].astype(jnp.float32).T.astype(jnp.bfloat16)

        @pl.loop(0, n, step=2, unroll=True)
        def _(block):
            before, here, after = taps[block], taps[block + 1], taps[block + 2]
            pair = jnp.concatenate(
                [
                    jnp.concatenate([before, here], axis=0),
                    jnp.concatenate([here, after], axis=0),
                ],
                axis=1,
            )
            both = dot(window_table[...], jnp.concatenate([pair, pair], axis=0))
            spec_filter[tile, block] = both[:, :chans]
            spec_filter[tile, block + 1] = both[:, chans:]

    def send_results(kind, source_of, target, slot, tile):
        @pl.loop(0, half)
        def _(step):
            index = turn(step)
            start(
                source_of(index),
                target.at[:, cols(mine, tile)],
                near_first + index,
                send_sem.at[kind, tile],
                result_sem.at[slot, tile, mine],
            )

        target[:, cols(mine, tile)] = source_of(mine)[...]

    def narrow_results(tile):
        @pl.when(lower)
        def _():
            narrow_in[tile, place] = value_loc[:, cols(mine, tile)]

        @pl.when(jnp.logical_not(lower))
        def _():
            narrow_in[tile, place] = grad_loc[:, cols(mine, tile)]

        wait_for(recv_sem.at[NARROW, tile], narrow_in.at[tile, pl.ds(0, half - 1)])
        spectrum(narrow_in, tile, 0)
        multiply_near(product_narrow, tile, jnp.where(lower, 1.0, -1.0))
        inverse(product_narrow, narrow_out, tile)

        @pl.when(lower)
        def _():
            send_results(RESULT_NARROW, lambda index: narrow_out.at[tile, index], conv_in, 0, tile)

        @pl.when(jnp.logical_not(lower))
        def _():
            send_results(RESULT_NARROW, lambda index: narrow_out.at[tile, half - 1 - index], back_in, 1, tile)

    def wide_near(tile):
        @pl.when(lower)
        def _():
            wide_in[tile, mirror] = grad_loc[:, cols(mine, tile)]

        @pl.when(jnp.logical_not(lower))
        def _():
            wide_in[tile, me] = value_loc[:, cols(mine, tile)]

        wait_for(recv_sem.at[WIDE_NEAR, tile], wide_in.at[tile, pl.ds(0, half - 1)])
        tile_sums(tile)
        spectrum(wide_in, tile, half)
        multiply_near(product_wide, tile, jnp.where(lower, -1.0, 1.0))

    def wide_results(tile):
        wait_for(recv_sem.at[WIDE_FAR, tile], wide_in.at[tile, pl.ds(0, half)])
        spectrum(wide_in, tile, 0)
        multiply_far(product_wide, tile, jnp.where(lower, -1.0, 1.0))
        inverse(product_wide, wide_out, tile)

        @pl.when(lower)
        def _():
            send_results(RESULT_WIDE, lambda index: wide_out.at[tile, half - 1 - index], back_in, 1, tile)

        @pl.when(jnp.logical_not(lower))
        def _():
            send_results(RESULT_WIDE, lambda index: wide_out.at[tile, index], conv_in, 0, tile)

    def tile_sums(tile):
        @pl.loop(0, rows // 16, init_carry=jnp.zeros((16, chans), jnp.float32))
        def total(step, carry):
            at = pl.ds(pl.multiple_of(step * 16, 16), 16)
            for block in range(half):
                carry += narrow_in[tile, block, at, :].astype(jnp.float32) * wide_in[
                    tile, n - 1 - block, at, :
                ].astype(jnp.float32)
            return carry

        sums_out[tile] = jnp.sum(total, axis=0, keepdims=True) * (1.0 / math.sqrt(length))
        sums_in[me, tile] = sums_out[tile]

        @pl.loop(0, n)
        def _(device):
            start(
                sums_out.at[tile],
                sums_in.at[me, tile],
                device,
                sums_send_sem.at[tile],
                sums_sem.at[me, tile],
            )

    for stage in (filter_spectra, narrow_results, wide_near, wide_results):
        pl.loop(0, 2)(stage)

    def finish_conv(at):
        cot_rows = cot_loc[:, at].astype(jnp.float32)
        gate_rows = gate_loc[:, at].astype(jnp.float32)
        mixed = conv_in[:, at].astype(jnp.float32) + skip[:, at] * value_loc[:, at].astype(
            jnp.float32
        )
        output[:, at] = (gate_rows * mixed).astype(jnp.bfloat16)
        gate_grad[:, at] = (cot_rows * mixed).astype(jnp.bfloat16)

    def finish_back(at):
        grads = grad_loc[:, at].astype(jnp.float32)
        value_grad[:, at] = (back_in[:, at].astype(jnp.float32) + skip[:, at] * grads).astype(
            jnp.bfloat16
        )

    def take(slot, landing, finish, tile):
        @pl.loop(0, half)
        def _(step):
            index = lax.rem(mine + step, half)
            at = cols(index, tile)
            other(
                near_first + index,
                lambda: wait_for(result_sem.at[slot, tile, index], landing.at[:, at]),
            )
            finish(at)

    def take_sums():
        @pl.loop(0, n)
        def _(device):
            for tile in range(2):
                other(
                    device,
                    lambda tile=tile: wait_for(sums_sem.at[device, tile], sums_in.at[device, tile]),
                )

        for index in range(half):
            for tile in range(2):
                sums_table[2 * index + tile] = sums_in[index, tile] + sums_in[half + index, tile]
        gain[...] = sums_table[owner[me]]

    for narrow in (True, False):

        @pl.loop(0, 2)
        def _(tile, narrow=narrow):
            @pl.when(lower if narrow else jnp.logical_not(lower))
            def _():
                take(0, conv_in, finish_conv, tile)

            @pl.when(jnp.logical_not(lower) if narrow else lower)
            def _():
                take(1, back_in, finish_back, tile)

            if narrow:
                for kind, count in (
                    (FILTER, n - 1),
                    (NARROW, half - 1),
                    (WIDE_NEAR, half - 1),
                    (WIDE_FAR, half),
                    (RESULT_NARROW, half - 1),
                ):
                    wait_for(send_sem.at[kind, tile], wide_in.at[tile, pl.ds(0, count)])
                wait_for(sums_send_sem.at[tile], sums_table.at[pl.ds(0, n - 1)])
            else:
                wait_for(send_sem.at[RESULT_WIDE, tile], wide_in.at[tile, pl.ds(0, half - 1)])

        if narrow:
            take_sums()


def finish_kernel(
    output_loc, value_grad_loc, gate_grad_loc, gain_loc, output, value_grad, gate_grad, gain, sem
):
    copies = [
        pltpu.make_async_copy(source, target, sem.at[index])
        for index, (source, target) in enumerate(
            (
                (output_loc, output),
                (value_grad_loc, value_grad),
                (gate_grad_loc, gate_grad),
                (gain_loc, gain),
            )
        )
    ]
    for copy in copies:
        copy.start()
    for copy in copies:
        copy.wait()


def fused_body(value, gate, long_filter, skip_gain, cotangent, owner_map):
    n = lax.axis_size("seq")
    rows, group = value.shape
    chans = group // n
    tables = block_tables(rows)
    anywhere = pl.BlockSpec(memory_space=pltpu.HBM)
    vmem = pl.BlockSpec(memory_space=pltpu.VMEM)
    bf16, f32 = jnp.bfloat16, jnp.float32
    half = n // 2
    half_spec = pltpu.VMEM((2, half, 2 * rows, chans), f32)
    tokens = pltpu.VMEM((rows, group), bf16)
    tiles = pltpu.VMEM((2, n, rows, chans), bf16)
    half_tiles = pltpu.VMEM((2, half, rows, chans), bf16)
    local = pl.pallas_call(
        functools.partial(fused_kernel, n),
        out_shape=(tokens, tokens, tokens, pltpu.VMEM((1, chans), f32)),
        in_specs=[anywhere] * 9,
        out_specs=(vmem,) * 4,
        scratch_shapes=[
            *(pltpu.VMEM(table.shape, bf16) for table in tables),
            pltpu.VMEM((1, group), f32),
            pltpu.SMEM(owner_map.shape, jnp.int32),
            tokens,
            tokens,
            tokens,
            tokens,
            pltpu.VMEM((2, n, chans, rows), bf16),
            half_tiles,
            tiles,
            pltpu.VMEM((n + 1, rows, chans), bf16),
            pltpu.VMEM((2, n, 2 * rows, chans), f32),
            pltpu.VMEM((half, 2 * rows, chans), f32),
            half_spec,
            half_spec,
            half_tiles,
            half_tiles,
            tokens,
            tokens,
            pltpu.VMEM((2, 1, chans), f32),
            pltpu.VMEM((n, 2, 1, chans), f32),
            pltpu.VMEM((n, 1, chans), f32),
            pltpu.SemaphoreType.DMA((KINDS, 2)),
            pltpu.SemaphoreType.DMA((KINDS, 2)),
            pltpu.SemaphoreType.DMA((2, 2, half)),
            pltpu.SemaphoreType.DMA((2,)),
            pltpu.SemaphoreType.DMA((n, 2)),
            pltpu.SemaphoreType.DMA((10,)),
        ],
        compiler_params=pltpu.CompilerParams(
            collective_id=0,
            has_side_effects=True,
            vmem_limit_bytes=DEVICE_VMEM - 6 * rows * group - 2**16,
        ),
    )(
        value,
        long_filter,
        gate,
        cotangent,
        skip_gain.reshape(1, group),
        owner_map,
        *tables,
    )
    result = jax.ShapeDtypeStruct((rows, group), bf16)
    output, value_grad, gate_grad, gain = pl.pallas_call(
        finish_kernel,
        out_shape=(result, result, result, jax.ShapeDtypeStruct((1, chans), f32)),
        in_specs=[vmem] * 4,
        out_specs=(anywhere,) * 4,
        scratch_shapes=[pltpu.SemaphoreType.DMA((4,))],
        compiler_params=pltpu.CompilerParams(vmem_limit_bytes=2**20),
    )(*local)
    return (output, value_grad, gate_grad, gain.reshape(1, 1, chans))


def body(value, gate, long_filter, skip_gain, cotangent, owner_map):
    n = lax.axis_size("seq")
    rows, group = value.shape
    aligned = rows % LANES == 0 and group % (n * LANES) == 0 and n % 4 == 0
    needed = 64 * rows * group + 48 * rows * rows
    chosen = fused_body if aligned and needed <= DEVICE_VMEM // 2 else split_body
    return chosen(value, gate, long_filter, skip_gain, cotangent, owner_map)


def solution(mesh):
    in_specs = (
        P("seq", "chan"),
        P("seq", "chan"),
        P("chan", "seq"),
        P("chan"),
        P("seq", "chan"),
        P(),
    )
    out_specs = (P("seq", "chan"), P("seq", "chan"), P("seq", "chan"), P("chan", "seq", None))
    return jax.shard_map(body, mesh=mesh, in_specs=in_specs, out_specs=out_specs, check_vma=False)
```
